512 devices in a mesh: row: 16 (over z), col: 8 (over x, core), rep: 4 (over y).
Axes of the slice: x: 4, y: 4, z: 16, core: 2. Of those that a mesh axis runs over, the one named last changes fastest.
Arguments:
- density: float32 [4096, 4096], P(('col', 'rep'), 'row'), may hold values from -0.25 to 1.25, as said below
- pattern: int32 [64, 9], replicated, may hold values from 0 to 63, as said below
- grid_order: int32 [64], replicated, may hold values from 0 to 63, as said below
Outputs:
- purified: float32 [4096, 4096], P(('col', 'rep'), 'row')
The draws below stay inside these ranges and needn't reach their ends.
Inputs may be any that keep to these rules, and one draw needn't show every extreme that they name: `pattern`: row r lists (r + d) mod 64 for one set of 9 distinct offsets d that holds 0 and is closed under negation modulo 64. `grid_order`: each block index appears once. `density`: Symmetric; zero outside the blocks that the pattern lists.
All inputs are finite; a program needn't handle non-finite values.
Results may differ from the reference program's by a relative error of at most 0.00016.
Values sent between devices are 32-bit elements; how exact they have to be, the bound alone decides.
A program may use at most 64 MiB of HBM per device.

```python
import math
import jax
import jax.numpy as jnp
from jax import lax

BLOCK = 64
ROW_NONZERO = 9
STEPS = 2
BLOCKS = 64


def pattern_parts(key):
    order = jax.random.permutation(jax.random.fold_in(key, 11), BLOCKS).astype(jnp.int32)
    chosen = jax.random.permutation(jax.random.fold_in(key, 12), BLOCKS // 2 - 1)[:(ROW_NONZERO - 1) // 2].astype(jnp.int32) + 1
    offsets = jnp.concatenate([jnp.zeros((1,), jnp.int32), chosen, BLOCKS - chosen]).astype(jnp.int32)
    return (order, offsets)


def draw_pattern(key, part):
    order, offsets = pattern_parts(key)
    every = jnp.arange(BLOCKS, dtype=jnp.int32)
    return ((every[:, None] + offsets[None, :]) % BLOCKS).astype(jnp.int32)


def draw_grid_order(key, part):
    order, offsets = pattern_parts(key)
    return order


def draw_density(key, part):
    order, offsets = pattern_parts(key)
    width = BLOCK * BLOCKS
    spread = 0.25 / math.sqrt(BLOCK * ROW_NONZERO)
    noise = jax.random.truncated_normal(jax.random.fold_in(key, 21), -4.0, 4.0, (width, width), jnp.float32)
    diagonal = jax.random.uniform(jax.random.fold_in(key, 22), (width,), jnp.float32, 0.1, 0.9)
    symmetric = (noise + noise.T) * (spread / math.sqrt(2.0))
    every = jnp.arange(BLOCKS, dtype=jnp.int32)
    distance = (every[None, :] - every[:, None]) % BLOCKS
    nearby = jnp.any(distance[:, :, None] == offsets[None, None, :], axis=2).astype(jnp.float32)
    nearby_cells = jnp.repeat(jnp.repeat(nearby, BLOCK, axis=0), BLOCK, axis=1)
    natural = nearby_cells * symmetric + jnp.diag(diagonal)
    cells = (order[:, None] * BLOCK + jnp.arange(BLOCK, dtype=jnp.int32)[None, :]).reshape(-1)
    return natural[cells][:, cells]


def setup_inputs(seed: int = 0) -> dict:
    key_of = jax.random.split(jax.random.key(seed), 4)
    density = draw_density(jax.random.fold_in(key_of[3], 71), 0)
    pattern = draw_pattern(jax.random.fold_in(key_of[3], 71), 0)
    grid_order = draw_grid_order(jax.random.fold_in(key_of[3], 71), 0)
    return {"density": density, "pattern": pattern, "grid_order": grid_order}


def reference(density, pattern, grid_order):
    listed = pattern[grid_order]
    hits = jnp.any(listed[:, :, None] == grid_order[None, None, :], axis=1)
    mask = jnp.repeat(jnp.repeat(hits.astype(jnp.float32), BLOCK, axis=0), BLOCK, axis=1)
    current = density
    for repeat in range(STEPS):
        square = jnp.dot(current, current, precision=lax.Precision.HIGHEST, preferred_element_type=jnp.float32)
        cube = jnp.dot(square, current, precision=lax.Precision.HIGHEST, preferred_element_type=jnp.float32)
        current = mask * (3.0 * square - 2.0 * cube)
    return current
```

```python
import jax
import jax.numpy as jnp
from jax import lax
from jax.experimental import pallas as pl
from jax.experimental.pallas import tpu as pltpu
from jax.sharding import PartitionSpec as P

MESH = pl.DeviceIdType.MESH
F32 = jnp.float32
PLANES = 16
DEVS = 32
NB = 64
ROWS = 9
PAIRS = 5
LANES = 128
HI = lax.Precision.HIGHEST
CHUNK = (PAIRS, 8, LANES)
BATCHES = [(0, 1)] + [(2 * b - 1, 2) for b in range(1, 8)] + [(15, 1)]


class Place:
    def __init__(self):
        self.r = lax.axis_index("row")
        self.c = lax.axis_index("col")
        self.p = lax.axis_index("rep")
        self.me = self.c * 4 + self.p
        self.jj = self.c % 4
        self.core = self.c % 2
        self.s = (self.c // 4) * 4 + self.p
        partner_c = self.c + 2 - 4 * ((self.c // 2) % 2)
        sibling_c = self.c + 1 - 2 * self.core
        self.jp = partner_c % 4
        self.js = sibling_c % 4
        self.jq = (partner_c + 1 - 2 * self.core) % 4
        self.partner = (self.r, partner_c, self.p)
        self.sibling = (self.r, sibling_c, self.p)

    def plane(self, d):
        return (self.r, d // 4, d % 4)

    def along(self, d):
        return (lax.rem(self.r + d + PLANES, PLANES), self.c, self.p)

    def slice_owner(self, s2):
        return (self.r, (s2 // 4) * 4 + self.jj, s2 % 4)

    def chip(self, t):
        d = lax.rem((self.c // 2) * 4 + self.p + t, 16)
        return d, (self.r, (d // 4) * 2 + self.core, d % 4)


def put(src, dst, ssem, rsem, dev):
    pltpu.make_async_remote_copy(
        src_ref=src, dst_ref=dst, send_sem=ssem, recv_sem=rsem, device_id=dev, device_id_type=MESH
    ).start()


def take(ref, sem):
    pltpu.make_async_copy(ref, ref, sem).wait()


def signal(dev):
    pl.semaphore_signal(pltpu.get_barrier_semaphore(), inc=1, device_id=dev, device_id_type=MESH)


def times(first, last, body):
    def step(t, carry):
        body(t)
        return carry

    lax.fori_loop(first, last, step, 0)


def scatter_kernel(dens, landed, send, recv):
    at = Place()
    times(1, DEVS, lambda t: signal(at.plane(lax.rem(at.me + t, DEVS))))
    pl.semaphore_wait(pltpu.get_barrier_semaphore(), DEVS - 1)

    def lanes(c):
        return pl.ds(pl.multiple_of(((c % 4) // 2) * LANES, LANES), LANES)

    mine = landed.at[pl.ds(2 * at.me, 2)]

    def one(t):
        d = lax.rem(at.me + t, DEVS)
        dc = d // 4
        put(dens.at[:, (dc // 4) * 4 + d % 4, :, lanes(dc)], mine, send, recv, at.plane(d))

    times(1, DEVS, one)
    landed[pl.ds(2 * at.me, 2)] = dens[:, at.s, :, lanes(at.c)]
    rest = landed.at[pl.ds(0, 2 * (DEVS - 1))]
    take(rest, recv)
    take(rest, send)


def column_reduce(at, ct, rs, send, recv):
    def one(u):
        s2 = lax.rem(at.s + u, 8)
        put(ct.at[s2], rs.at[at.s], send, recv, at.slice_owner(s2))

    times(1, 8, one)
    rs[at.s] = ct[at.s]
    take(rs.at[pl.ds(0, 7)], recv)


def updated(sq, rs, t):
    acc = rs[0, t]
    for k in range(1, 8):
        acc = acc + rs[k, t]
    return 3.0 * sq[t] - 2.0 * acc


def meet_neighbours(at):
    for d in (1, -1, 2, -2):
        signal(at.along(d))
    times(1, 8, lambda u: signal(at.slice_owner(lax.rem(at.s + u, 8))))
    signal(at.partner)
    signal(at.sibling)
    pl.semaphore_wait(pltpu.get_barrier_semaphore(), 13)


def spread(at, own, x, bbuf, z_send, z_recv, par_send, par_recv, sib_send, sib_recv, b_send, b_recv):
    mine = x.at[at.jj]
    for d, o in ((1, 1), (-1, 2), (2, 3), (-2, 4)):
        put(own, mine.at[o], z_send, z_recv.at[o], at.along(d))

    def column(u):
        put(own, bbuf.at[at.s], b_send, b_recv, at.slice_owner(lax.rem(at.s + u, 8)))

    times(1, 8, column)
    put(own, mine.at[0], par_send, par_recv.at[0], at.partner)
    put(own, mine.at[0], sib_send.at[0], sib_recv.at[0], at.sibling)
    x[at.jj, 0] = own[...]
    bbuf[at.s] = own[...]

    def relay(b):
        part = x.at[at.jp, pl.ds(*BATCHES[b])]
        take(part, par_recv.at[b])
        put(part, part, sib_send.at[1], sib_recv.at[1], at.sibling)

    for b in range(1, 9):
        first, n = BATCHES[b]
        for o in range(first, first + n):
            take(mine.at[o], z_recv.at[o])
            if o + 4 <= 15:
                put(mine.at[o], mine.at[o + 4], z_send, z_recv.at[o + 4], at.along(2 if o % 2 == 1 else -2))
        part = mine.at[pl.ds(first, n)]
        put(part, part, par_send, par_recv.at[b], at.partner)
        put(part, part, sib_send.at[0], sib_recv.at[0], at.sibling)
        if b >= 3:
            relay(b - 3)
    for b in range(6, 9):
        relay(b)
    take(bbuf.at[pl.ds(0, 7)], b_recv)
    take(x.at[at.js], sib_recv.at[0])
    take(x.at[at.jq], sib_recv.at[1])
    take(mine.at[pl.ds(0, 15)], z_send)
    take(mine, par_send)
    take(mine, sib_send.at[0])
    take(mine, sib_send.at[1])
    take(bbuf.at[pl.ds(0, 7)], b_send)


def first_spread_kernel(own, x, bbuf, *sems):
    at = Place()
    meet_neighbours(at)
    spread(at, own, x, bbuf, *sems)


def next_spread_kernel(ct, sq, x, bbuf, rs, own, rs_send, rs_recv, *sems):
    at = Place()
    meet_neighbours(at)
    column_reduce(at, ct, rs, rs_send, rs_recv)
    for t in range(PAIRS):
        own[t] = updated(sq, rs, t)
    spread(at, own, x, bbuf, *sems)
    take(rs.at[pl.ds(0, 7)], rs_send)


def gather_kernel(ct, sq, full, rs, own, rs_send, rs_recv, send, recv, sib_send, sib_recv):
    at = Place()
    times(1, 16, lambda t: signal(at.chip(t)[1]))
    signal(at.sibling)
    pl.semaphore_wait(pltpu.get_barrier_semaphore(), 16)
    column_reduce(at, ct, rs, rs_send, rs_recv)
    for t in range(PAIRS):
        own[t] = updated(sq, rs, t)
    slot = at.core * 16 + (at.c // 2) * 4 + at.p

    def one(t):
        put(own, full.at[slot], send, recv.at[t], at.chip(t)[1])

    times(1, 16, one)
    put(own, full.at[slot], sib_send, sib_recv, at.sibling)
    full[slot] = own[...]

    def forward(t):
        d = lax.rem((at.c // 2) * 4 + at.p + 16 - t, 16)
        part = full.at[at.core * 16 + d]
        take(part, recv.at[t])
        put(part, part, sib_send, sib_recv, at.sibling)

    times(1, 16, forward)
    theirs = full.at[pl.ds((1 - at.core) * 16, 16)]
    take(theirs, sib_recv)
    take(theirs, sib_send)
    take(full.at[pl.ds(0, 15)], send)
    take(rs.at[pl.ds(0, 7)], rs_send)


def low_half():
    return lax.broadcasted_iota(jnp.int32, (8, LANES), 1) < 64


def turn(v):
    return pltpu.roll(v, 64, 1)


def compact_kernel(landed, pat, order, own, inv, pos, place):
    at = Place()
    low = low_half()

    def clear(o):
        inv[o] = jnp.int32(ROWS)

    times(0, NB, clear)

    def locate(q):
        place[order[q]] = q

    times(0, NB, locate)
    nj = order[4 * at.r + at.jj]
    for a in range(ROWS):
        off = pat[0, a]
        inv[off] = jnp.int32(a)
        pos[a] = place[(nj + off) & (NB - 1)]
    for t in range(PAIRS):
        v0 = landed[pos[2 * t]]
        lo = jnp.where(at.core == 0, v0, turn(v0))
        if 2 * t + 1 < ROWS:
            v1 = landed[pos[2 * t + 1]]
            hi = jnp.where(at.core == 1, v1, turn(v1))
        else:
            hi = jnp.zeros_like(v0)
        own[t] = jnp.where(low, lo, hi)


def product_kernel(x, bbuf, pat, inv, pos, ct, sq, xa, g, bm, tt):
    at = Place()
    low = low_half()
    zero = jnp.zeros((8, LANES), F32)
    offs = [pat[0, a] for a in range(ROWS)]
    for t in range(PAIRS):
        for k in range(8):
            v = bbuf[k, t]
            bm[128 * t + 8 * k:128 * t + 8 * k + 8] = v[:, :64]
            bm[128 * t + 64 + 8 * k:128 * t + 72 + 8 * k] = v[:, 64:]
    for a in range(ROWS):
        i = pos[a]
        ahead = (at.r - (i >> 2)) & (PLANES - 1)
        o = jnp.where(ahead == 0, 0, jnp.where(ahead <= 8, 2 * ahead - 1, 2 * (PLANES - ahead)))
        keep = low if a % 2 == 0 else jnp.logical_not(low)
        for t in range(PAIRS):
            v = x[i & 3, o, t]
            for h in range(2):
                xa[a * 10 + 2 * t + h] = jnp.where(keep, v if h == a % 2 else turn(v), zero)

    def rows_of(k):
        row = pl.multiple_of(8 * k, 8)
        for t in range(PAIRS):
            v = xa[20 * t + inv[(k - offs[2 * t]) & (NB - 1)]]
            if 2 * t + 1 < ROWS:
                v = v + xa[20 * t + 10 + inv[(k - offs[2 * t + 1]) & (NB - 1)]]
            g[pl.ds(row, 8), t * LANES:(t + 1) * LANES] = v

    times(0, NB, rows_of)
    tmat = jnp.dot(g[...], bm[...], precision=HI, preferred_element_type=F32)
    tt[...] = jnp.concatenate([tmat, tmat], axis=1)
    cube = jnp.dot(tmat.T, g[...], precision=HI, preferred_element_type=F32)
    for t in range(PAIRS):
        w = cube[:, t * LANES:(t + 1) * LANES].T
        w = jnp.concatenate([w[:64], w[64:]], axis=1)
        for k in range(8):
            ct[k, t] = w[8 * k:8 * k + 8]
        sq0 = tt[pl.ds(pl.multiple_of(8 * offs[2 * t], 8), 8)]
        sq1 = zero
        if 2 * t + 1 < ROWS:
            sq1 = tt[pl.ds(pl.multiple_of(8 * offs[2 * t + 1], 8), 8)]
        sq[t] = jnp.where(low, sq0, sq1)


def tile_kernel(full, order, inv, out):
    at = Place()
    low = low_half()
    for b in range(2):
        ni = order[2 * at.me + b]
        for hp in range(2):
            find = [inv[(ni - order[4 * at.r + 2 * hp + q]) & (NB - 1)] for q in range(2)]
            for k in range(8):
                got = []
                for q in range(2):
                    v = full[16 * q + (2 * (k // 4) + hp) * 4 + k % 4, find[q] >> 1]
                    got.append(jnp.where((find[q] & 1) == q, v, turn(v)))
                out[b, k, :, hp * LANES:(hp + 1) * LANES] = jnp.where(low, got[0], got[1])


VM = pl.BlockSpec(memory_space=pltpu.VMEM)
SM = pl.BlockSpec(memory_space=pltpu.SMEM)
DMA = pltpu.SemaphoreType.DMA
SPREAD_SEMS = [DMA, DMA((PLANES,)), DMA, DMA((9,)), DMA((2,)), DMA((2,)), DMA, DMA]


def shape(*dims):
    return jax.ShapeDtypeStruct(dims, F32)


def call(body, ident, in_specs, out_shape, scratch, out_specs=None):
    extra = {} if ident is None else {"collective_id": ident, "has_side_effects": True}
    return pl.pallas_call(
        body,
        out_shape=out_shape,
        in_specs=in_specs,
        out_specs=out_specs or jax.tree.map(lambda _: VM, out_shape),
        scratch_shapes=scratch,
        compiler_params=pltpu.CompilerParams(**extra),
    )


def local(density, pattern, grid_order):
    landed = call(scatter_kernel, 0, [VM], shape(NB, 8, LANES), [DMA, DMA])(density.reshape(2, 8, 8, 256))
    own, inv, pos = call(
        compact_kernel, None, [VM, SM, SM],
        (shape(*CHUNK), jax.ShapeDtypeStruct((NB,), jnp.int32), jax.ShapeDtypeStruct((ROWS,), jnp.int32)),
        [pltpu.SMEM((NB,), jnp.int32)], (VM, SM, SM),
    )(landed, pattern, grid_order)
    spread_out = (shape(4, PLANES, *CHUNK), shape(8, *CHUNK))
    x, bbuf = call(first_spread_kernel, 1, [VM], spread_out, SPREAD_SEMS)(own)
    product = call(
        product_kernel, None, [VM, VM, SM, SM, SM], (shape(8, *CHUNK), shape(*CHUNK)),
        [
            pltpu.VMEM((ROWS * 10, 8, LANES), F32),
            pltpu.VMEM((NB * 8, PAIRS * LANES), F32),
            pltpu.VMEM((PAIRS * LANES, 64), F32),
            pltpu.VMEM((NB * 8, LANES), F32),
        ],
    )
    ct, sq = product(x, bbuf, pattern, inv, pos)
    sums = [pltpu.VMEM((8, *CHUNK), F32), pltpu.VMEM(CHUNK, F32), DMA, DMA]
    x, bbuf = call(next_spread_kernel, 2, [VM, VM], spread_out, sums + SPREAD_SEMS)(ct, sq)
    ct, sq = product(x, bbuf, pattern, inv, pos)
    full = call(gather_kernel, 3, [VM, VM], shape(DEVS, *CHUNK), sums + [DMA, DMA((16,)), DMA, DMA])(ct, sq)
    out = call(tile_kernel, None, [VM, SM, SM], shape(2, 8, 8, 256), [])(full, grid_order, inv)
    return out.reshape(128, 256)


def solution(mesh):
    in_specs = (P(("col", "rep"), "row"), P(), P())
    out_specs = P(("col", "rep"), "row")
    return jax.shard_map(local, mesh=mesh, in_specs=in_specs, out_specs=out_specs, check_vma=False)
```

```python
import jax
import jax.numpy as jnp
from jax import lax
from jax.experimental import pallas as pl
from jax.experimental.pallas import tpu as pltpu
from jax.sharding import PartitionSpec as P

MESH = pl.DeviceIdType.MESH
F32 = jnp.float32
BF16 = jnp.bfloat16
PLANES = 16
CHIPS = 16
DEVS = 32
NB = 64
ROWS = 9
PAIRS = 5
LANES = 128
WIDE = PAIRS * LANES
CHUNK = (PAIRS, 8, LANES)
POS = NB
OFF = POS + 2 * ROWS
TABLE = 96

PARENT = {1: 0, 2: 0, 4: 0, 3: 4, 5: 4, 6: 4, 7: 4, 8: 4}
FIRST = (4, 2, 1)
ONWARD = (8, 7, 6, 3, 5)
ARRIVAL = (1, 2, 4, 5, 3, 6, 7, 8)
REACH = {1: 8, -1: 7}
JUMPS = (1, 2, 3, 4)


class Place:
    def __init__(self):
        self.r = lax.axis_index("row")
        self.c = lax.axis_index("col")
        self.p = lax.axis_index("rep")
        self.me = self.c * 4 + self.p
        self.core = self.c % 2
        self.chip = (self.c // 2) * 4 + self.p
        self.sibling = (self.r, self.c + 1 - 2 * self.core, self.p)

    def plane(self, d):
        return (self.r, d // 4, d % 4)

    def along(self, d):
        return (lax.rem(self.r + d + PLANES, PLANES), self.c, self.p)

    def other(self, t):
        d = lax.rem(self.chip + t, CHIPS)
        return d, (self.r, (d // 4) * 2 + self.core, d % 4)


def put(src, dst, ssem, rsem, dev):
    pltpu.make_async_remote_copy(
        src_ref=src, dst_ref=dst, send_sem=ssem, recv_sem=rsem, device_id=dev, device_id_type=MESH
    ).start()


def take(ref, sem):
    pltpu.make_async_copy(ref, ref, sem).wait()


def signal(dev):
    pl.semaphore_signal(pltpu.get_barrier_semaphore(), inc=1, device_id=dev, device_id_type=MESH)


def met(n):
    pl.semaphore_wait(pltpu.get_barrier_semaphore(), n)


def times(first, last, body):
    def step(t, carry):
        body(t)
        return carry

    lax.fori_loop(first, last, step, 0)


def greet_along(at):
    for d in JUMPS:
        signal(at.along(d))
        signal(at.along(-d))


def lane_low():
    return lax.broadcasted_iota(jnp.int32, (8, LANES), 1) < 64


def row_low():
    return lax.broadcasted_iota(jnp.int32, (8, LANES), 0) < 4


def turn(v):
    return pltpu.roll(v, 64, 1)


def flip(v):
    return pltpu.roll(v, 4, 0)


def quadrants(q00, q01, q10, q11):
    low = lane_low()
    return jnp.where(row_low(), jnp.where(low, q00, q01), jnp.where(low, q10, q11))


def spread(at, own, x, bbuf, z_send, z_recv, sib_send, sib_recv, b_send, b_recv):
    mine = x.at[at.core]

    def slot(sign, q):
        return 2 * q - 1 if sign > 0 else 2 * q

    def send(src, sign, q):
        o = slot(sign, q)
        put(src, mine.at[o], z_send, z_recv.at[o], at.along(sign * (q - PARENT[q])))

    for q in FIRST:
        for sign in (1, -1):
            send(own, sign, q)

    def column(t):
        put(own, bbuf.at[at.chip], b_send, b_recv, at.other(t)[1])

    put(own, mine.at[0], sib_send, sib_recv, at.sibling)
    times(1, CHIPS, column)
    x[at.core, 0] = own[...]
    bbuf[at.chip] = own[...]
    for q in ARRIVAL:
        signs = [sign for sign in (1, -1) if q <= REACH[sign]]
        for sign in signs:
            part = mine.at[slot(sign, q)]
            take(part, z_recv.at[slot(sign, q)])
            for k in ONWARD:
                if PARENT[k] == q and k <= REACH[sign]:
                    send(part, sign, k)
        for sign in signs:
            part = mine.at[slot(sign, q)]
            put(part, part, sib_send, sib_recv, at.sibling)
    take(bbuf.at[pl.ds(0, CHIPS - 1)], b_recv)
    take(x.at[1 - at.core], sib_recv)
    take(mine.at[pl.ds(0, PLANES - 1)], z_send)
    take(mine, sib_send)
    take(bbuf.at[pl.ds(0, CHIPS - 1)], b_send)


def first_kernel(dens, tab, x, bbuf, landed, own, p_send, p_recv, *sems):
    at = Place()
    times(1, DEVS, lambda t: signal(at.plane(lax.rem(at.me + t, DEVS))))
    greet_along(at)
    met(DEVS - 1 + 2 * len(JUMPS))

    def lanes(c):
        return pl.ds(pl.multiple_of((c % 2) * LANES, LANES), LANES)

    def one(t):
        d = lax.rem(at.me + t, DEVS)
        dc = d // 4
        tile_row = (dc // 2) * 2 + (d % 4) // 2
        put(dens.at[:, tile_row, :, lanes(dc)], landed.at[pl.ds(2 * at.me, 2)], p_send, p_recv, at.plane(d))

    times(1, DEVS, one)
    landed[pl.ds(2 * at.me, 2)] = dens[:, at.chip // 2, :, lanes(at.c)]
    rest = landed.at[pl.ds(0, 2 * (DEVS - 1))]
    take(rest, p_recv)
    for t in range(PAIRS):
        parts = []
        for q in range(2):
            for h in range(2):
                a = 2 * t + h
                if a == ROWS:
                    parts.append(jnp.zeros((8, LANES), F32))
                    continue
                v = landed[tab[POS + q * ROWS + a]]
                v = v if h == q else turn(v)
                parts.append(jnp.where(at.p % 2 == q, v, flip(v)))
        own[t] = quadrants(*parts)
    spread(at, own, x, bbuf, *sems)
    take(rest, p_send)


def reduce_slices(at, ct, sq, rs, own, send, recv):
    def one(t):
        d, dev = at.other(t)
        put(ct.at[d], rs.at[at.chip], send, recv, dev)

    times(1, CHIPS, one)
    rs[at.chip] = ct[at.chip]
    take(rs.at[pl.ds(0, CHIPS - 1)], recv)
    for t in range(PAIRS):
        acc = rs[0, t]
        for k in range(1, CHIPS):
            acc = acc + rs[k, t]
        own[t] = 3.0 * sq[t] - 2.0 * acc


def next_kernel(ct, sq, x, bbuf, rs, own, rs_send, rs_recv, *sems):
    at = Place()
    times(1, CHIPS, lambda t: signal(at.other(t)[1]))
    signal(at.sibling)
    greet_along(at)
    met(CHIPS + 2 * len(JUMPS))
    reduce_slices(at, ct, sq, rs, own, rs_send, rs_recv)
    spread(at, own, x, bbuf, *sems)
    take(rs.at[pl.ds(0, CHIPS - 1)], rs_send)


def last_kernel(ct, sq, order, tab, out, rs, own, dup, fsend, frecv, rs_send, rs_recv, send, recv):
    at = Place()
    times(1, DEVS, lambda t: signal(at.plane(lax.rem(at.me + t, DEVS))))
    met(DEVS - 1)
    reduce_slices(at, ct, sq, rs, own, rs_send, rs_recv)
    low = lane_low()
    for t in range(PAIRS):
        v = own[t]
        w = turn(v)
        dup[2 * t] = jnp.where(low, v, w)
        dup[2 * t + 1] = jnp.where(low, w, v)
    n0 = order[4 * at.r + 2 * at.core]
    n1 = order[4 * at.r + 2 * at.core + 1]

    def dense(d):
        parts = [dup[tab[(order[2 * d + b] - n) & (NB - 1)]] for n in (n0, n1) for b in range(2)]
        fsend[d] = quadrants(*parts)

    times(0, DEVS, dense)

    def give(t):
        d = lax.rem(at.me + t, DEVS)
        put(fsend.at[d], frecv.at[at.chip * 2 + at.core], send, recv, at.plane(d))

    times(1, DEVS, give)
    frecv[at.chip * 2 + at.core] = fsend[at.me]
    rest = frecv.at[pl.ds(0, DEVS - 1)]
    take(rest, recv)
    for b in range(2):
        for w in range(8):
            for h in range(2):
                parts = []
                for sp in range(2):
                    for q in range(2):
                        v = frecv[(2 * w + sp) * 2 + h]
                        v = v if q == b else turn(v)
                        parts.append(v if q == sp else flip(v))
                out[b, w, :, h * LANES:(h + 1) * LANES] = quadrants(*parts)
    take(rest, send)
    take(rs.at[pl.ds(0, CHIPS - 1)], rs_send)


def table_kernel(pat, order, tab, place):
    at = Place()
    for o in range(NB):
        tab[o] = jnp.int32(ROWS)
    for q in range(NB):
        place[order[q]] = jnp.int32(q)
    for a in range(ROWS):
        off = pat[a, 0]
        tab[off] = jnp.int32(a)
        tab[OFF + a] = off
        for q in range(2):
            tab[POS + q * ROWS + a] = place[(order[4 * at.r + 2 * at.core + q] + off) & (NB - 1)]


def split(v):
    hi = v.astype(BF16)
    return hi, (v - hi.astype(F32)).astype(BF16)


def dot3(a, b):
    def one(u, v):
        return jnp.dot(u, v, preferred_element_type=F32)

    return one(a[0], b[0]) + (one(a[0], b[1]) + one(a[1], b[0]))


def product_kernel(x, bbuf, tab, ct, sq, xa, ghi, glo, bm, tt, wide):
    at = Place()
    low = lane_low()
    top = row_low()
    offs = [tab[OFF + a] for a in range(ROWS)]
    for q in range(2):
        for a in range(ROWS):
            i = tab[POS + q * ROWS + a]
            ahead = (at.r - (i >> 2)) & (PLANES - 1)
            o = jnp.where(ahead == 0, 0, jnp.where(ahead <= 8, 2 * ahead - 1, 2 * (PLANES - ahead)))
            lane_keep = low if a % 2 == 0 else jnp.logical_not(low)
            even = jnp.logical_and(lane_keep, top)
            odd = jnp.logical_and(lane_keep, jnp.logical_not(top))
            for t in range(PAIRS):
                v = x[(i >> 1) & 1, o, t]
                f = flip(v)
                first = (i & 1) == 0
                e = jnp.where(first, v, f)
                d = jnp.where(first, f, v)
                for h in range(2):
                    same = h == a % 2
                    xa[q, 0, a * 10 + 2 * t + h] = jnp.where(even, e if same else turn(e), 0.0)
                    xa[q, 1, a * 10 + 2 * t + h] = jnp.where(odd, d if same else turn(d), 0.0)

    for q in range(2):
        for t in range(PAIRS):
            for w in range(8):
                u, v = bbuf[2 * w, t], bbuf[2 * w + 1, t]
                v = jnp.where(top, u, flip(v)) if q == 0 else jnp.where(top, flip(u), v)
                bm[q, 128 * t + 8 * w:128 * t + 8 * w + 8] = v[:, :64]
                bm[q, 128 * t + 64 + 8 * w:128 * t + 72 + 8 * w] = v[:, 64:]

    def rows_of(u):
        row = pl.multiple_of(16 * u, 16)
        for t in range(PAIRS):
            index = []
            for k in range(4):
                pair = [2 * t, 2 * t + 1] if 2 * t + 1 < ROWS else [2 * t]
                index.append([10 * a + tab[(4 * u + k - offs[a]) & (NB - 1)] for a in pair])
            for q in range(2):
                tiles = []
                for k in (0, 2):
                    v = xa[q, 0, index[k][0]] + xa[q, 1, index[k + 1][0]]
                    if len(index[k]) == 2:
                        v = v + (xa[q, 0, index[k][1]] + xa[q, 1, index[k + 1][1]])
                    tiles.append(v)
                hi, lo = split(jnp.concatenate(tiles, axis=0))
                ghi[q, pl.ds(row, 16), t * LANES:(t + 1) * LANES] = hi
                glo[q, pl.ds(row, 16), t * LANES:(t + 1) * LANES] = lo

    times(0, NB // 4, rows_of)
    for q in range(2):
        g = (ghi[q], glo[q])
        tmat = dot3(g, split(bm[q]))
        tt[q] = jnp.concatenate([tmat, tmat], axis=1).reshape(32, 8, LANES)
        cube = dot3(split(tmat.T), g)
        for t in range(PAIRS):
            w = cube[:, t * LANES:(t + 1) * LANES].T
            wide[q, t] = jnp.concatenate([w[:64], w[64:]], axis=1).reshape(8, 8, LANES)
    for t in range(PAIRS):
        for w in range(8):
            u, v = wide[0, t, w], wide[1, t, w]
            ct[2 * w, t] = jnp.where(top, u, flip(v))
            ct[2 * w + 1, t] = jnp.where(top, flip(u), v)
        parts = []
        for q in range(2):
            for h in range(2):
                a = 2 * t + h
                if a == ROWS:
                    parts.append(jnp.zeros((8, LANES), F32))
                    continue
                v = tt[q, offs[a] >> 1]
                parts.append(jnp.where((offs[a] & 1) == q, v, flip(v)))
        sq[t] = quadrants(*parts)


VM = pl.BlockSpec(memory_space=pltpu.VMEM)
SM = pl.BlockSpec(memory_space=pltpu.SMEM)
DMA = pltpu.SemaphoreType.DMA
SPREAD_SEMS = [DMA, DMA((PLANES,)), DMA, DMA, DMA, DMA]


def shape(*dims, dtype=F32):
    return jax.ShapeDtypeStruct(dims, dtype)


def vmem(*dims, dtype=F32):
    return pltpu.VMEM(dims, dtype)


def call(body, ident, in_specs, out_shape, scratch, out_specs=None):
    extra = {} if ident is None else {"collective_id": ident, "has_side_effects": True}
    return pl.pallas_call(
        body,
        out_shape=out_shape,
        in_specs=in_specs,
        out_specs=out_specs or jax.tree.map(lambda _: VM, out_shape),
        scratch_shapes=scratch,
        compiler_params=pltpu.CompilerParams(**extra),
    )


def local(density, pattern, grid_order):
    tab = call(
        table_kernel, None, [SM, SM], shape(TABLE, dtype=jnp.int32), [pltpu.SMEM((NB,), jnp.int32)], SM
    )(pattern.T, grid_order)
    spread_out = (shape(2, PLANES, *CHUNK), shape(CHIPS, *CHUNK))
    x, bbuf = call(
        first_kernel, 0, [VM, SM], spread_out, [vmem(NB, 8, LANES), vmem(*CHUNK), DMA, DMA] + SPREAD_SEMS
    )(density.reshape(2, 8, 8, 256), tab)
    product = call(
        product_kernel, None, [VM, VM, SM], (shape(CHIPS, *CHUNK), shape(*CHUNK)),
        [
            vmem(2, 2, ROWS * 10, 8, LANES),
            vmem(2, 4 * NB, WIDE, dtype=BF16),
            vmem(2, 4 * NB, WIDE, dtype=BF16),
            vmem(2, WIDE, 64),
            vmem(2, 32, 8, LANES),
            vmem(2, PAIRS, 8, 8, LANES),
        ],
    )
    ct, sq = product(x, bbuf, tab)
    sums = [vmem(CHIPS, *CHUNK), vmem(*CHUNK)]
    x, bbuf = call(next_kernel, 1, [VM, VM], spread_out, sums + [DMA, DMA] + SPREAD_SEMS)(ct, sq)
    ct, sq = product(x, bbuf, tab)
    out = call(
        last_kernel, 2, [VM, VM, SM, SM], shape(2, 8, 8, 256),
        sums + [vmem(10, 8, LANES), vmem(DEVS, 8, LANES), vmem(DEVS, 8, LANES), DMA, DMA, DMA, DMA],
    )(ct, sq, grid_order, tab)
    return out.reshape(128, 256)


def solution(mesh):
    in_specs = (P(("col", "rep"), "row"), P(), P())
    out_specs = P(("col", "rep"), "row")
    return jax.shard_map(local, mesh=mesh, in_specs=in_specs, out_specs=out_specs, check_vma=False)
```

```python
import jax
import jax.numpy as jnp
from jax import lax
from jax.experimental import pallas as pl
from jax.experimental.pallas import tpu as pltpu
from jax.sharding import PartitionSpec as P

MESH = pl.DeviceIdType.MESH
F32 = jnp.float32
BF16 = jnp.bfloat16
PLANES = 16
CHIPS = 16
DEVS = 32
NB = 64
ROWS = 9
PAIRS = 5
LANES = 128
WIDE = PAIRS * LANES
CHUNK = (PAIRS, 8, LANES)
POS = NB
OFF = POS + 2 * ROWS
TABLE = 96

PARENT = {1: 0, 2: 0, 4: 0, 3: 4, 5: 4, 6: 4, 7: 4, 8: 4}
FIRST = (4, 2, 1)
ONWARD = (8, 7, 6, 3, 5)
ARRIVAL = (1, 2, 4, 5, 3, 6, 7, 8)
REACH = {1: 8, -1: 7}
JUMPS = (1, 2, 3, 4)


class Place:
    def __init__(self):
        self.r = lax.axis_index("row")
        self.c = lax.axis_index("col")
        self.p = lax.axis_index("rep")
        self.me = self.c * 4 + self.p
        self.core = self.c % 2
        self.chip = (self.c // 2) * 4 + self.p
        self.sibling = (self.r, self.c + 1 - 2 * self.core, self.p)

    def plane(self, d):
        return (self.r, d // 4, d % 4)

    def along(self, d):
        return (lax.rem(self.r + d + PLANES, PLANES), self.c, self.p)

    def other(self, t):
        d = lax.rem(self.chip + t, CHIPS)
        return d, (self.r, (d // 4) * 2 + self.core, d % 4)


def put(src, dst, ssem, rsem, dev):
    pltpu.make_async_remote_copy(
        src_ref=src, dst_ref=dst, send_sem=ssem, recv_sem=rsem, device_id=dev, device_id_type=MESH
    ).start()


def take(ref, sem):
    pltpu.make_async_copy(ref, ref, sem).wait()


def signal(dev):
    pl.semaphore_signal(pltpu.get_barrier_semaphore(), inc=1, device_id=dev, device_id_type=MESH)


def met(n):
    pl.semaphore_wait(pltpu.get_barrier_semaphore(), n)


def times(first, last, body):
    def step(t, carry):
        body(t)
        return carry

    lax.fori_loop(first, last, step, 0)


def greet_along(at):
    for d in JUMPS:
        signal(at.along(d))
        signal(at.along(-d))


def lane_low():
    return lax.broadcasted_iota(jnp.int32, (8, LANES), 1) < 64


def row_low():
    return lax.broadcasted_iota(jnp.int32, (8, LANES), 0) < 4


def turn(v):
    return pltpu.roll(v, 64, 1)


def flip(v):
    return pltpu.roll(v, 4, 0)


def quadrants(q00, q01, q10, q11):
    low = lane_low()
    return jnp.where(row_low(), jnp.where(low, q00, q01), jnp.where(low, q10, q11))


def spread(at, own, x, bbuf, z_send, z_recv, sib_send, sib_recv, b_send, b_recv):
    mine = x.at[at.core]

    def slot(sign, q):
        return 2 * q - 1 if sign > 0 else 2 * q

    def send(src, sign, q):
        o = slot(sign, q)
        put(src, mine.at[o], z_send, z_recv.at[o], at.along(sign * (q - PARENT[q])))

    for q in FIRST:
        for sign in (1, -1):
            send(own, sign, q)

    def column(t):
        put(own, bbuf.at[at.chip], b_send, b_recv, at.other(t)[1])

    put(own, mine.at[0], sib_send, sib_recv, at.sibling)
    times(1, CHIPS, column)
    x[at.core, 0] = own[...]
    bbuf[at.chip] = own[...]
    for q in ARRIVAL:
        signs = [sign for sign in (1, -1) if q <= REACH[sign]]
        for sign in signs:
            part = mine.at[slot(sign, q)]
            take(part, z_recv.at[slot(sign, q)])
            for k in ONWARD:
                if PARENT[k] == q and k <= REACH[sign]:
                    send(part, sign, k)
        for sign in signs:
            part = mine.at[slot(sign, q)]
            put(part, part, sib_send, sib_recv, at.sibling)
    take(bbuf.at[pl.ds(0, CHIPS - 1)], b_recv)
    take(x.at[1 - at.core], sib_recv)


def scatter(at, dens, tab, landed, own, p_send, p_recv):
    def lanes(c):
        return pl.ds(pl.multiple_of((c % 2) * LANES, LANES), LANES)

    def one(t):
        d = lax.rem(at.me + t, DEVS)
        dc = d // 4
        tile_row = (dc // 2) * 2 + (d % 4) // 2
        put(dens.at[:, tile_row, :, lanes(dc)], landed.at[pl.ds(2 * at.me, 2)], p_send, p_recv, at.plane(d))

    times(1, DEVS, one)
    landed[pl.ds(2 * at.me, 2)] = dens[:, at.chip // 2, :, lanes(at.c)]
    take(landed.at[pl.ds(0, 2 * (DEVS - 1))], p_recv)
    for t in range(PAIRS):
        parts = []
        for q in range(2):
            for h in range(2):
                a = 2 * t + h
                if a == ROWS:
                    parts.append(jnp.zeros((8, LANES), F32))
                    continue
                v = landed[tab[POS + q * ROWS + a]]
                v = v if h == q else turn(v)
                parts.append(jnp.where(at.p % 2 == q, v, flip(v)))
        own[t] = quadrants(*parts)


def reduce_slices(at, ct, sq, rs, own, send, recv):
    def one(t):
        d, dev = at.other(t)
        put(ct.at[d], rs.at[at.chip], send, recv, dev)

    times(1, CHIPS, one)
    rs[at.chip] = ct[at.chip]
    take(rs.at[pl.ds(0, CHIPS - 1)], recv)
    for t in range(PAIRS):
        acc = rs[0, t]
        for k in range(1, CHIPS):
            acc = acc + rs[k, t]
        own[t] = 3.0 * sq[t] - 2.0 * acc


def finish(at, order, tab, out, own, dup, fsend, frecv, send, recv):
    low = lane_low()
    for t in range(PAIRS):
        v = own[t]
        w = turn(v)
        dup[2 * t] = jnp.where(low, v, w)
        dup[2 * t + 1] = jnp.where(low, w, v)
    n0 = order[4 * at.r + 2 * at.core]
    n1 = order[4 * at.r + 2 * at.core + 1]

    def dense(d):
        parts = [dup[tab[(order[2 * d + b] - n) & (NB - 1)]] for n in (n0, n1) for b in range(2)]
        fsend[d] = quadrants(*parts)

    times(0, DEVS, dense)

    def give(t):
        d = lax.rem(at.me + t, DEVS)
        put(fsend.at[d], frecv.at[at.chip * 2 + at.core], send, recv, at.plane(d))

    times(1, DEVS, give)
    frecv[at.chip * 2 + at.core] = fsend[at.me]
    rest = frecv.at[pl.ds(0, DEVS - 1)]
    take(rest, recv)
    for b in range(2):
        for w in range(8):
            for h in range(2):
                parts = []
                for sp in range(2):
                    for q in range(2):
                        v = frecv[(2 * w + sp) * 2 + h]
                        v = v if q == b else turn(v)
                        parts.append(v if q == sp else flip(v))
                out[b, w, :, h * LANES:(h + 1) * LANES] = quadrants(*parts)


def table_kernel(pat, order, tab, place):
    at = Place()
    for o in range(NB):
        tab[o] = jnp.int32(ROWS)
    for q in range(NB):
        place[order[q]] = jnp.int32(q)
    for a in range(ROWS):
        off = pat[a, 0]
        tab[off] = jnp.int32(a)
        tab[OFF + a] = off
        for q in range(2):
            tab[POS + q * ROWS + a] = place[(order[4 * at.r + 2 * at.core + q] + off) & (NB - 1)]


def split(v):
    hi = v.astype(BF16)
    return hi, (v - hi.astype(F32)).astype(BF16)


def dot3(a, b):
    def one(u, v):
        return jnp.dot(u, v, preferred_element_type=F32)

    return one(a[0], b[0]) + (one(a[0], b[1]) + one(a[1], b[0]))


def product(at, x, bbuf, tab, ct, sq, xa, ghi, glo, bm, tt, wide):
    low = lane_low()
    top = row_low()
    offs = [tab[OFF + a] for a in range(ROWS)]
    for q in range(2):
        for a in range(ROWS):
            i = tab[POS + q * ROWS + a]
            ahead = (at.r - (i >> 2)) & (PLANES - 1)
            o = jnp.where(ahead == 0, 0, jnp.where(ahead <= 8, 2 * ahead - 1, 2 * (PLANES - ahead)))
            lane_keep = low if a % 2 == 0 else jnp.logical_not(low)
            even = jnp.logical_and(lane_keep, top)
            odd = jnp.logical_and(lane_keep, jnp.logical_not(top))
            for t in range(PAIRS):
                v = x[(i >> 1) & 1, o, t]
                f = flip(v)
                first = (i & 1) == 0
                e = jnp.where(first, v, f)
                d = jnp.where(first, f, v)
                for h in range(2):
                    same = h == a % 2
                    xa[q, 0, a * 10 + 2 * t + h] = jnp.where(even, e if same else turn(e), 0.0)
                    xa[q, 1, a * 10 + 2 * t + h] = jnp.where(odd, d if same else turn(d), 0.0)

    for q in range(2):
        for t in range(PAIRS):
            for w in range(8):
                u, v = bbuf[2 * w, t], bbuf[2 * w + 1, t]
                v = jnp.where(top, u, flip(v)) if q == 0 else jnp.where(top, flip(u), v)
                bm[q, 128 * t + 8 * w:128 * t + 8 * w + 8] = v[:, :64]
                bm[q, 128 * t + 64 + 8 * w:128 * t + 72 + 8 * w] = v[:, 64:]

    def rows_of(u):
        row = pl.multiple_of(16 * u, 16)
        for t in range(PAIRS):
            index = []
            for k in range(4):
                pair = [2 * t, 2 * t + 1] if 2 * t + 1 < ROWS else [2 * t]
                index.append([10 * a + tab[(4 * u + k - offs[a]) & (NB - 1)] for a in pair])
            for q in range(2):
                tiles = []
                for k in (0, 2):
                    v = xa[q, 0, index[k][0]] + xa[q, 1, index[k + 1][0]]
                    if len(index[k]) == 2:
                        v = v + (xa[q, 0, index[k][1]] + xa[q, 1, index[k + 1][1]])
                    tiles.append(v)
                hi, lo = split(jnp.concatenate(tiles, axis=0))
                ghi[q, pl.ds(row, 16), t * LANES:(t + 1) * LANES] = hi
                glo[q, pl.ds(row, 16), t * LANES:(t + 1) * LANES] = lo

    times(0, NB // 4, rows_of)
    for q in range(2):
        g = (ghi[q], glo[q])
        tmat = dot3(g, split(bm[q]))
        tt[q] = jnp.concatenate([tmat, tmat], axis=1).reshape(32, 8, LANES)
        cube = dot3(split(tmat.T), g)
        for t in range(PAIRS):
            w = cube[:, t * LANES:(t + 1) * LANES].T
            wide[q, t] = jnp.concatenate([w[:64], w[64:]], axis=1).reshape(8, 8, LANES)
    for t in range(PAIRS):
        for w in range(8):
            u, v = wide[0, t, w], wide[1, t, w]
            ct[2 * w, t] = jnp.where(top, u, flip(v))
            ct[2 * w + 1, t] = jnp.where(top, flip(u), v)
        parts = []
        for q in range(2):
            for h in range(2):
                a = 2 * t + h
                if a == ROWS:
                    parts.append(jnp.zeros((8, LANES), F32))
                    continue
                v = tt[q, offs[a] >> 1]
                parts.append(jnp.where((offs[a] & 1) == q, v, flip(v)))
        sq[t] = quadrants(*parts)


def kernel(
    dens, order, tab, out,
    landed, own, x_a, x_b, bbuf, ct, sq, rs, xa, ghi, glo, bm, tt, wide, dup, fsend, frecv,
    p_send, p_recv, z_send, z_recv, sib_send, sib_recv, b_send, b_recv, rs_send, rs_recv, f_send, f_recv,
):
    at = Place()
    x = (x_a, x_b)
    times(1, DEVS, lambda t: signal(at.plane(lax.rem(at.me + t, DEVS))))
    greet_along(at)
    met(DEVS - 1 + 2 * len(JUMPS))
    scatter(at, dens, tab, landed, own.at[0], p_send, p_recv)
    for k in range(2):
        spread(
            at, own.at[k], x[k], bbuf.at[k], z_send.at[k], z_recv.at[k], sib_send.at[k], sib_recv.at[k],
            b_send.at[k], b_recv.at[k],
        )
        product(at, x[k], bbuf.at[k], tab, ct.at[k], sq, xa, ghi, glo, bm, tt, wide)
        reduce_slices(at, ct.at[k], sq, rs.at[k], own.at[k + 1], rs_send.at[k], rs_recv.at[k])
    finish(at, order, tab, out, own.at[2], dup, fsend, frecv, f_send, f_recv)
    take(landed.at[pl.ds(0, 2 * (DEVS - 1))], p_send)
    for k in range(2):
        take(x[k].at[0, pl.ds(0, PLANES - 1)], z_send.at[k])
        take(x[k].at[0], sib_send.at[k])
        take(bbuf.at[k, pl.ds(0, CHIPS - 1)], b_send.at[k])
        take(rs.at[k, pl.ds(0, CHIPS - 1)], rs_send.at[k])
    take(frecv.at[pl.ds(0, DEVS - 1)], f_send)


VM = pl.BlockSpec(memory_space=pltpu.VMEM)
SM = pl.BlockSpec(memory_space=pltpu.SMEM)
DMA = pltpu.SemaphoreType.DMA


def vmem(*dims, dtype=F32):
    return pltpu.VMEM(dims, dtype)


def local(density, pattern, grid_order):
    tab = pl.pallas_call(
        table_kernel,
        out_shape=jax.ShapeDtypeStruct((TABLE,), jnp.int32),
        in_specs=[SM, SM],
        out_specs=SM,
        scratch_shapes=[pltpu.SMEM((NB,), jnp.int32)],
    )(pattern.T, grid_order)
    out = pl.pallas_call(
        kernel,
        out_shape=jax.ShapeDtypeStruct((2, 8, 8, 256), F32),
        in_specs=[VM, SM, SM],
        out_specs=VM,
        scratch_shapes=[
            vmem(NB, 8, LANES), vmem(3, *CHUNK),
            vmem(2, PLANES, *CHUNK), vmem(2, PLANES, *CHUNK), vmem(2, CHIPS, *CHUNK), vmem(2, CHIPS, *CHUNK), vmem(*CHUNK),
            vmem(2, CHIPS, *CHUNK),
            vmem(2, 2, ROWS * 10, 8, LANES), vmem(2, 4 * NB, WIDE, dtype=BF16), vmem(2, 4 * NB, WIDE, dtype=BF16),
            vmem(2, WIDE, 64), vmem(2, 32, 8, LANES), vmem(2, PAIRS, 8, 8, LANES),
            vmem(10, 8, LANES), vmem(DEVS, 8, LANES), vmem(DEVS, 8, LANES),
            DMA, DMA, DMA((2,)), DMA((2, PLANES)), DMA((2,)), DMA((2,)), DMA((2,)), DMA((2,)), DMA((2,)), DMA((2,)),
            DMA, DMA,
        ],
        compiler_params=pltpu.CompilerParams(collective_id=0, has_side_effects=True),
    )(density.reshape(2, 8, 8, 256), grid_order, tab)
    return out.reshape(128, 256)


def solution(mesh):
    in_specs = (P(("col", "rep"), "row"), P(), P())
    out_specs = P(("col", "rep"), "row")
    return jax.shard_map(local, mesh=mesh, in_specs=in_specs, out_specs=out_specs, check_vma=False)
```

```python
import jax
import jax.numpy as jnp
from jax import lax
from jax.experimental import pallas as pl
from jax.experimental.pallas import tpu as pltpu
from jax.sharding import PartitionSpec as P

MESH = pl.DeviceIdType.MESH
F32 = jnp.float32
BF16 = jnp.bfloat16
PLANES = 16
CHIPS = 16
DEVS = 32
NB = 64
ROWS = 9
PAIRS = 5
LANES = 128
WIDE = PAIRS * LANES
CHUNK = (PAIRS, 8, LANES)
POS = NB
OFF = POS + 2 * ROWS
TABLE = 96

PARENT = {1: 0, 2: 0, 4: 0, 3: 4, 5: 4, 6: 4, 7: 4}
FIRST = (4, 2, 1)
ONWARD = (7, 6, 3, 5)
ARRIVAL = (1, 2, 4, 5, 3, 6, 7)
JUMPS = (4, 3, 2, 1)
SPOTS = sorted(
    ((dx, dy) for dx in range(4) for dy in range(4) if dx or dy),
    key=lambda o: -(min(o[0], 4 - o[0]) + min(o[1], 4 - o[1])),
)


class Place:
    def __init__(self):
        self.r = lax.axis_index("row")
        self.c = lax.axis_index("col")
        self.p = lax.axis_index("rep")
        self.me = self.c * 4 + self.p
        self.core = self.c % 2
        self.chip = (self.c // 2) * 4 + self.p
        self.sibling = (self.r, self.c + 1 - 2 * self.core, self.p)

    def along(self, d):
        return (lax.rem(self.r + d + PLANES, PLANES), self.c, self.p)

    def spot(self, dx, dy):
        return lax.rem(self.c // 2 + dx, 4), lax.rem(self.p + dy, 4)

    def other(self, o):
        x, y = self.spot(*o)
        return x * 4 + y, (self.r, x * 2 + self.core, y)

    def cores(self):
        for dx, dy in SPOTS:
            x, y = self.spot(dx, dy)
            for h in range(2):
                yield x, y, h, (self.r, x * 2 + h, y)
        yield self.c // 2, self.p, 1 - self.core, self.sibling


def put(src, dst, ssem, rsem, dev):
    pltpu.make_async_remote_copy(
        src_ref=src, dst_ref=dst, send_sem=ssem, recv_sem=rsem, device_id=dev, device_id_type=MESH
    ).start()


def take(ref, sem):
    pltpu.make_async_copy(ref, ref, sem).wait()


def signal(dev):
    pl.semaphore_signal(pltpu.get_barrier_semaphore(), inc=1, device_id=dev, device_id_type=MESH)


def met(n):
    pl.semaphore_wait(pltpu.get_barrier_semaphore(), n)


def times(first, last, body):
    def step(t, carry):
        body(t)
        return carry

    lax.fori_loop(first, last, step, 0)


def greet_along(at):
    for d in JUMPS:
        signal(at.along(d))
        signal(at.along(-d))


def lane_low():
    return lax.broadcasted_iota(jnp.int32, (8, LANES), 1) < 64


def row_low():
    return lax.broadcasted_iota(jnp.int32, (8, LANES), 0) < 4


def turn(v):
    return pltpu.roll(v, 64, 1)


def flip(v):
    return pltpu.roll(v, 4, 0)


def quadrants(q00, q01, q10, q11):
    low = lane_low()
    return jnp.where(row_low(), jnp.where(low, q00, q01), jnp.where(low, q10, q11))


def spread(at, own, x, bbuf, z_send, z_recv, sib_send, sib_recv, b_send, b_recv):
    mine = x.at[at.core]

    def slot(sign, q):
        return 2 * q - 1 if sign > 0 else 2 * q

    def send(src, sign, q):
        o = slot(sign, q)
        put(src, mine.at[o], z_send, z_recv.at[o], at.along(sign * (q - PARENT[q])))

    for q in FIRST:
        for sign in (1, -1):
            send(own, sign, q)

    for o in SPOTS:
        put(own, bbuf.at[at.chip], b_send, b_recv, at.other(o)[1])
    put(own, mine.at[0], sib_send, sib_recv, at.sibling)
    x[at.core, 0] = own[...]
    bbuf[at.chip] = own[...]
    side = 1 - 2 * at.core
    for q in ARRIVAL:
        for sign in (1, -1):
            part = mine.at[slot(sign, q)]
            take(part, z_recv.at[slot(sign, q)])
            for k in ONWARD:
                if PARENT[k] == q:
                    send(part, sign, k)
        if q == 4:
            put(mine.at[7 + at.core], mine.at[15], z_send, z_recv.at[15], at.along(4 * side))
        for sign in (1, -1):
            part = mine.at[slot(sign, q)]
            put(part, part, sib_send, sib_recv, at.sibling)
    last = mine.at[15]
    take(last, z_recv.at[15])
    put(last, last, sib_send, sib_recv, at.sibling)
    take(bbuf.at[pl.ds(0, CHIPS - 1)], b_recv)
    take(x.at[1 - at.core], sib_recv)


def fill_tables(at, pat, order, tab):
    offs = [pat[a, 0] for a in range(ROWS)]
    targets = [(order[4 * at.r + 2 * at.core + q] + off) & (NB - 1) for q in range(2) for off in offs]

    def step(o, found):
        v = jnp.int32(ROWS)
        for a in range(ROWS):
            v = jnp.where(offs[a] == o, jnp.int32(a), v)
        tab[o] = v
        n = order[o]
        return tuple(jnp.where(n == target, o, f) for target, f in zip(targets, found))

    found = lax.fori_loop(0, NB, step, (jnp.int32(0),) * len(targets))
    for k, f in enumerate(found):
        tab[POS + k] = f
    for a in range(ROWS):
        tab[OFF + a] = offs[a]


def scatter(at, dens, pat, order, tab, landed, own, p_send, p_recv):
    def lanes(c):
        return pl.ds(pl.multiple_of((c % 2) * LANES, LANES), LANES)

    for x, y, h, dev in at.cores():
        put(dens.at[:, x * 2 + y // 2, :, lanes(h)], landed.at[pl.ds(2 * at.me, 2)], p_send, p_recv, dev)
    fill_tables(at, pat, order, tab)
    landed[pl.ds(2 * at.me, 2)] = dens[:, at.chip // 2, :, lanes(at.c)]
    take(landed.at[pl.ds(0, 2 * (DEVS - 1))], p_recv)
    for t in range(PAIRS):
        parts = []
        for q in range(2):
            for h in range(2):
                a = 2 * t + h
                if a == ROWS:
                    parts.append(jnp.zeros((8, LANES), F32))
                    continue
                v = landed[tab[POS + q * ROWS + a]]
                v = v if h == q else turn(v)
                parts.append(jnp.where(at.p % 2 == q, v, flip(v)))
        own[t] = quadrants(*parts)


def reduce_slices(at, ct, sq, rs, own, send, recv):
    for o in SPOTS:
        d, dev = at.other(o)
        put(ct.at[d], rs.at[at.chip], send, recv, dev)
    rs[at.chip] = ct[at.chip]
    take(rs.at[pl.ds(0, CHIPS - 1)], recv)
    for t in range(PAIRS):
        acc = rs[0, t]
        for k in range(1, CHIPS):
            acc = acc + rs[k, t]
        own[t] = 3.0 * sq[t] - 2.0 * acc


def finish(at, order, tab, out, own, dup, fsend, frecv, send, recv):
    low = lane_low()
    for t in range(PAIRS):
        v = own[t]
        w = turn(v)
        dup[2 * t] = jnp.where(low, v, w)
        dup[2 * t + 1] = jnp.where(low, w, v)
    n0 = order[4 * at.r + 2 * at.core]
    n1 = order[4 * at.r + 2 * at.core + 1]

    def dense(d):
        parts = [dup[tab[(order[2 * d + b] - n) & (NB - 1)]] for n in (n0, n1) for b in range(2)]
        fsend[d] = quadrants(*parts)

    times(0, DEVS, dense)

    for x, y, h, dev in at.cores():
        put(fsend.at[(x * 2 + h) * 4 + y], frecv.at[at.chip * 2 + at.core], send, recv, dev)
    frecv[at.chip * 2 + at.core] = fsend[at.me]
    rest = frecv.at[pl.ds(0, DEVS - 1)]
    take(rest, recv)
    for b in range(2):
        for w in range(8):
            for h in range(2):
                parts = []
                for sp in range(2):
                    for q in range(2):
                        v = frecv[(2 * w + sp) * 2 + h]
                        v = v if q == b else turn(v)
                        parts.append(v if q == sp else flip(v))
                out[b, w, :, h * LANES:(h + 1) * LANES] = quadrants(*parts)


def split(v):
    hi = v.astype(BF16)
    return hi, (v - hi.astype(F32)).astype(BF16)


def dot3(a, b):
    def one(u, v):
        return jnp.dot(u, v, preferred_element_type=F32)

    return one(a[0], b[0]) + (one(a[0], b[1]) + one(a[1], b[0]))


def product(at, x, bbuf, tab, ct, sq, xa, ghi, glo, bm, tt, wide):
    low = lane_low()
    top = row_low()
    offs = [tab[OFF + a] for a in range(ROWS)]
    for q in range(2):
        for a in range(ROWS):
            i = tab[POS + q * ROWS + a]
            ahead = (at.r - (i >> 2)) & (PLANES - 1)
            o = jnp.where(ahead == 0, 0, jnp.where(ahead <= 8, 2 * ahead - 1, 2 * (PLANES - ahead)))
            lane_keep = low if a % 2 == 0 else jnp.logical_not(low)
            even = jnp.logical_and(lane_keep, top)
            odd = jnp.logical_and(lane_keep, jnp.logical_not(top))
            for t in range(PAIRS):
                v = x[(i >> 1) & 1, o, t]
                f = flip(v)
                first = (i & 1) == 0
                e = jnp.where(first, v, f)
                d = jnp.where(first, f, v)
                for h in range(2):
                    same = h == a % 2
                    xa[q, 0, a * 10 + 2 * t + h] = jnp.where(even, e if same else turn(e), 0.0)
                    xa[q, 1, a * 10 + 2 * t + h] = jnp.where(odd, d if same else turn(d), 0.0)

    for q in range(2):
        for t in range(PAIRS):
            for w in range(8):
                u, v = bbuf[2 * w, t], bbuf[2 * w + 1, t]
                v = jnp.where(top, u, flip(v)) if q == 0 else jnp.where(top, flip(u), v)
                bm[q, 128 * t + 8 * w:128 * t + 8 * w + 8] = v[:, :64]
                bm[q, 128 * t + 64 + 8 * w:128 * t + 72 + 8 * w] = v[:, 64:]

    def rows_of(u):
        row = pl.multiple_of(16 * u, 16)
        for t in range(PAIRS):
            index = []
            for k in range(4):
                pair = [2 * t, 2 * t + 1] if 2 * t + 1 < ROWS else [2 * t]
                index.append([10 * a + tab[(4 * u + k - offs[a]) & (NB - 1)] for a in pair])
            for q in range(2):
                tiles = []
                for k in (0, 2):
                    v = xa[q, 0, index[k][0]] + xa[q, 1, index[k + 1][0]]
                    if len(index[k]) == 2:
                        v = v + (xa[q, 0, index[k][1]] + xa[q, 1, index[k + 1][1]])
                    tiles.append(v)
                hi, lo = split(jnp.concatenate(tiles, axis=0))
                ghi[q, pl.ds(row, 16), t * LANES:(t + 1) * LANES] = hi
                glo[q, pl.ds(row, 16), t * LANES:(t + 1) * LANES] = lo

    times(0, NB // 4, rows_of)
    for q in range(2):
        g = (ghi[q], glo[q])
        tmat = dot3(g, split(bm[q]))
        tt[q] = jnp.concatenate([tmat, tmat], axis=1).reshape(32, 8, LANES)
        cube = dot3(split(tmat.T), g)
        for t in range(PAIRS):
            w = cube[:, t * LANES:(t + 1) * LANES].T
            wide[q, t] = jnp.concatenate([w[:64], w[64:]], axis=1).reshape(8, 8, LANES)
    for t in range(PAIRS):
        for w in range(8):
            u, v = wide[0, t, w], wide[1, t, w]
            ct[2 * w, t] = jnp.where(top, u, flip(v))
            ct[2 * w + 1, t] = jnp.where(top, flip(u), v)
        parts = []
        for q in range(2):
            for h in range(2):
                a = 2 * t + h
                if a == ROWS:
                    parts.append(jnp.zeros((8, LANES), F32))
                    continue
                v = tt[q, offs[a] >> 1]
                parts.append(jnp.where((offs[a] & 1) == q, v, flip(v)))
        sq[t] = quadrants(*parts)


def kernel(
    dens, pat, order, out,
    tab, landed, own, x_a, x_b, bbuf, ct, sq, rs, xa, ghi, glo, bm, tt, wide, dup, fsend, frecv,
    p_send, p_recv, z_send, z_recv, sib_send, sib_recv, b_send, b_recv, rs_send, rs_recv, f_send, f_recv,
):
    at = Place()
    x = (x_a, x_b)
    greet_along(at)
    for *_, dev in at.cores():
        signal(dev)
    met(DEVS - 1 + 2 * len(JUMPS))
    scatter(at, dens, pat, order, tab, landed, own.at[0], p_send, p_recv)
    for k in range(2):
        spread(
            at, own.at[k], x[k], bbuf.at[k], z_send.at[k], z_recv.at[k], sib_send.at[k], sib_recv.at[k],
            b_send.at[k], b_recv.at[k],
        )
        product(at, x[k], bbuf.at[k], tab, ct.at[k], sq, xa, ghi, glo, bm, tt, wide)
        reduce_slices(at, ct.at[k], sq, rs.at[k], own.at[k + 1], rs_send.at[k], rs_recv.at[k])
    finish(at, order, tab, out, own.at[2], dup, fsend, frecv, f_send, f_recv)
    take(landed.at[pl.ds(0, 2 * (DEVS - 1))], p_send)
    for k in range(2):
        take(x[k].at[0, pl.ds(0, PLANES - 1)], z_send.at[k])
        take(x[k].at[0], sib_send.at[k])
        take(bbuf.at[k, pl.ds(0, CHIPS - 1)], b_send.at[k])
        take(rs.at[k, pl.ds(0, CHIPS - 1)], rs_send.at[k])
    take(frecv.at[pl.ds(0, DEVS - 1)], f_send)


VM = pl.BlockSpec(memory_space=pltpu.VMEM)
SM = pl.BlockSpec(memory_space=pltpu.SMEM)
DMA = pltpu.SemaphoreType.DMA


def vmem(*dims, dtype=F32):
    return pltpu.VMEM(dims, dtype)


def local(density, pattern, grid_order):
    out = pl.pallas_call(
        kernel,
        out_shape=jax.ShapeDtypeStruct((2, 8, 8, 256), F32),
        in_specs=[VM, SM, SM],
        out_specs=VM,
        scratch_shapes=[
            pltpu.SMEM((TABLE,), jnp.int32),
            vmem(NB, 8, LANES), vmem(3, *CHUNK),
            vmem(2, PLANES, *CHUNK), vmem(2, PLANES, *CHUNK), vmem(2, CHIPS, *CHUNK), vmem(2, CHIPS, *CHUNK), vmem(*CHUNK),
            vmem(2, CHIPS, *CHUNK),
            vmem(2, 2, ROWS * 10, 8, LANES), vmem(2, 4 * NB, WIDE, dtype=BF16), vmem(2, 4 * NB, WIDE, dtype=BF16),
            vmem(2, WIDE, 64), vmem(2, 32, 8, LANES), vmem(2, PAIRS, 8, 8, LANES),
            vmem(10, 8, LANES), vmem(DEVS, 8, LANES), vmem(DEVS, 8, LANES),
            DMA, DMA, DMA((2,)), DMA((2, PLANES)), DMA((2,)), DMA((2,)), DMA((2,)), DMA((2,)), DMA((2,)), DMA((2,)),
            DMA, DMA,
        ],
        compiler_params=pltpu.CompilerParams(collective_id=0, has_side_effects=True, vmem_limit_bytes=16 << 20),
    )(density.reshape(2, 8, 8, 256), pattern.T, grid_order)
    return out.reshape(128, 256)


def solution(mesh):
    in_specs = (P(("col", "rep"), "row"), P(), P())
    out_specs = P(("col", "rep"), "row")
    return jax.shard_map(local, mesh=mesh, in_specs=in_specs, out_specs=out_specs, check_vma=False)
```

```python
import jax
import jax.numpy as jnp
from jax import lax
from jax.experimental import pallas as pl
from jax.experimental.pallas import tpu as pltpu
from jax.sharding import PartitionSpec as P

MESH = pl.DeviceIdType.MESH
F32 = jnp.float32
BF16 = jnp.bfloat16
PLANES = 16
CHIPS = 16
DEVS = 32
NB = 64
ROWS = 9
PAIRS = 5
LANES = 128
WIDE = PAIRS * LANES
CHUNK = (PAIRS, 8, LANES)
POS = NB
OFF = POS + 2 * ROWS
TABLE = 96

PARENT = {1: 0, 2: 0, 4: 0, 3: 4, 5: 4, 6: 4, 7: 4}
FIRST = (4, 2, 1)
ONWARD = (7, 6, 3, 5)
ARRIVAL = (1, 2, 4, 5, 3, 6, 7)
JUMPS = (4, 3, 2, 1)
SPOTS = sorted(
    ((dx, dy) for dx in range(4) for dy in range(4) if dx or dy),
    key=lambda o: -(min(o[0], 4 - o[0]) + min(o[1], 4 - o[1])),
)


class Place:
    def __init__(self):
        self.r = lax.axis_index("row")
        self.c = lax.axis_index("col")
        self.p = lax.axis_index("rep")
        self.me = self.c * 4 + self.p
        self.core = self.c % 2
        self.chip = (self.c // 2) * 4 + self.p
        self.sibling = (self.r, self.c + 1 - 2 * self.core, self.p)

    def along(self, d):
        return (lax.rem(self.r + d + PLANES, PLANES), self.c, self.p)

    def spot(self, dx, dy):
        return lax.rem(self.c // 2 + dx, 4), lax.rem(self.p + dy, 4)

    def other(self, o):
        x, y = self.spot(*o)
        return x * 4 + y, (self.r, x * 2 + self.core, y)

    def cores(self):
        for dx, dy in SPOTS:
            x, y = self.spot(dx, dy)
            for h in range(2):
                yield x, y, h, (self.r, x * 2 + h, y)
        yield self.c // 2, self.p, 1 - self.core, self.sibling


def put(src, dst, ssem, rsem, dev):
    pltpu.make_async_remote_copy(
        src_ref=src, dst_ref=dst, send_sem=ssem, recv_sem=rsem, device_id=dev, device_id_type=MESH
    ).start()


def take(ref, sem):
    pltpu.make_async_copy(ref, ref, sem).wait()


def signal(dev):
    pl.semaphore_signal(pltpu.get_barrier_semaphore(), inc=1, device_id=dev, device_id_type=MESH)


def met(n):
    pl.semaphore_wait(pltpu.get_barrier_semaphore(), n)


def times(first, last, body):
    def step(t, carry):
        body(t)
        return carry

    lax.fori_loop(first, last, step, 0)


def greet_along(at):
    for d in JUMPS:
        signal(at.along(d))
        signal(at.along(-d))


def lane_low():
    return lax.broadcasted_iota(jnp.int32, (8, LANES), 1) < 64


def row_low():
    return lax.broadcasted_iota(jnp.int32, (8, LANES), 0) < 4


def turn(v):
    return pltpu.roll(v, 64, 1)


def flip(v):
    return pltpu.roll(v, 4, 0)


def quadrants(q00, q01, q10, q11):
    low = lane_low()
    return jnp.where(row_low(), jnp.where(low, q00, q01), jnp.where(low, q10, q11))


def block_columns(bbuf, bm):
    top = row_low()
    for q in range(2):
        for t in range(PAIRS):
            for w in range(8):
                u, v = bbuf[2 * w, t], bbuf[2 * w + 1, t]
                v = jnp.where(top, u, flip(v)) if q == 0 else jnp.where(top, flip(u), v)
                bm[q, 128 * t + 8 * w:128 * t + 8 * w + 8] = v[:, :64]
                bm[q, 128 * t + 64 + 8 * w:128 * t + 72 + 8 * w] = v[:, 64:]


def spread(at, own, x, bbuf, bm, z_send, z_recv, sib_send, sib_recv, b_send, b_recv):
    mine = x.at[at.core]

    def slot(sign, q):
        return 2 * q - 1 if sign > 0 else 2 * q

    def send(src, sign, q):
        o = slot(sign, q)
        put(src, mine.at[o], z_send, z_recv.at[o], at.along(sign * (q - PARENT[q])))

    for q in FIRST:
        for sign in (1, -1):
            send(own, sign, q)

    for o in SPOTS:
        put(own, bbuf.at[at.chip], b_send, b_recv, at.other(o)[1])
    put(own, mine.at[0], sib_send, sib_recv, at.sibling)
    x[at.core, 0] = own[...]
    bbuf[at.chip] = own[...]
    side = 1 - 2 * at.core
    for q in ARRIVAL:
        for sign in (1, -1):
            part = mine.at[slot(sign, q)]
            take(part, z_recv.at[slot(sign, q)])
            for k in ONWARD:
                if PARENT[k] == q:
                    send(part, sign, k)
        if q == 4:
            put(mine.at[7 + at.core], mine.at[15], z_send, z_recv.at[15], at.along(4 * side))
        for sign in (1, -1):
            part = mine.at[slot(sign, q)]
            put(part, part, sib_send, sib_recv, at.sibling)
        if q == 4:
            take(bbuf.at[pl.ds(0, CHIPS - 1)], b_recv)
            block_columns(bbuf, bm)
    last = mine.at[15]
    take(last, z_recv.at[15])
    put(last, last, sib_send, sib_recv, at.sibling)
    take(x.at[1 - at.core], sib_recv)


def fill_tables(at, pat, order, tab):
    offs = [pat[a, 0] for a in range(ROWS)]
    targets = [(order[4 * at.r + 2 * at.core + q] + off) & (NB - 1) for q in range(2) for off in offs]

    def step(o, found):
        v = jnp.int32(ROWS)
        for a in range(ROWS):
            v = jnp.where(offs[a] == o, jnp.int32(a), v)
        tab[o] = v
        n = order[o]
        return tuple(jnp.where(n == target, o, f) for target, f in zip(targets, found))

    found = lax.fori_loop(0, NB, step, (jnp.int32(0),) * len(targets))
    for k, f in enumerate(found):
        tab[POS + k] = f
    for a in range(ROWS):
        tab[OFF + a] = offs[a]


def scatter(at, dens, pat, order, tab, landed, own, tables, load, p_send, p_recv):
    def lanes(c):
        return pl.ds(pl.multiple_of((c % 2) * LANES, LANES), LANES)

    own_part = pltpu.make_async_copy(
        dens.at[:, at.chip // 2, pl.ds(4 * (at.p % 2), 4), lanes(at.c)], landed.at[pl.ds(2 * at.me, 2)], load
    )
    own_part.start()
    for x, y, h, dev in at.cores():
        put(dens.at[:, x * 2 + y // 2, pl.ds(4 * (y % 2), 4), lanes(h)], landed.at[pl.ds(2 * at.me, 2)], p_send, p_recv, dev)
    for copy in (*tables, own_part):
        copy.wait()
    fill_tables(at, pat, order, tab)
    take(landed.at[pl.ds(0, 2 * (DEVS - 1))], p_recv)
    for t in range(PAIRS):
        parts = []
        for q in range(2):
            for h in range(2):
                a = 2 * t + h
                if a == ROWS:
                    parts.append(jnp.zeros((8, LANES), F32))
                    continue
                v = landed[tab[POS + q * ROWS + a]]
                v = jnp.concatenate([v, v], axis=0)
                parts.append(v if h == q else turn(v))
        own[t] = quadrants(*parts)


def reduce_slices(at, ct, sq, rs, own, send, recv):
    for o in SPOTS:
        d, dev = at.other(o)
        put(ct.at[d], rs.at[at.chip], send, recv, dev)
    rs[at.chip] = ct[at.chip]
    take(rs.at[pl.ds(0, CHIPS - 1)], recv)
    for t in range(PAIRS):
        acc = rs[0, t]
        for k in range(1, CHIPS):
            acc = acc + rs[k, t]
        own[t] = 3.0 * sq[t] - 2.0 * acc


def finish(at, order, tab, out, own, dup, fsend, frecv, send, recv):
    low = lane_low()
    for t in range(PAIRS):
        v = own[t]
        w = turn(v)
        dup[2 * t] = jnp.where(low, v, w)
        dup[2 * t + 1] = jnp.where(low, w, v)
    n0 = order[4 * at.r + 2 * at.core]
    n1 = order[4 * at.r + 2 * at.core + 1]

    def dense(d):
        parts = [dup[tab[(order[2 * d + b] - n) & (NB - 1)]] for n in (n0, n1) for b in range(2)]
        fsend[d] = quadrants(*parts)

    times(0, DEVS, dense)

    for x, y, h, dev in at.cores():
        put(fsend.at[(x * 2 + h) * 4 + y], frecv.at[at.chip * 2 + at.core], send, recv, dev)
    frecv[at.chip * 2 + at.core] = fsend[at.me]
    rest = frecv.at[pl.ds(0, DEVS - 1)]
    take(rest, recv)
    for b in range(2):
        for w in range(8):
            for h in range(2):
                parts = []
                for sp in range(2):
                    for q in range(2):
                        v = frecv[(2 * w + sp) * 2 + h]
                        v = v if q == b else turn(v)
                        parts.append(v if q == sp else flip(v))
                out[b, w, :, h * LANES:(h + 1) * LANES] = quadrants(*parts)


def split(v):
    hi = v.astype(BF16)
    return hi, (v - hi.astype(F32)).astype(BF16)


def dot3(a, b):
    def one(u, v):
        return jnp.dot(u, v, preferred_element_type=F32)

    return one(a[0], b[0]) + (one(a[0], b[1]) + one(a[1], b[0]))


def product(at, x, tab, ct, sq, xa, ghi, glo, bm, tt, wide):
    low = lane_low()
    top = row_low()
    offs = [tab[OFF + a] for a in range(ROWS)]
    for q in range(2):
        for a in range(ROWS):
            i = tab[POS + q * ROWS + a]
            ahead = (at.r - (i >> 2)) & (PLANES - 1)
            o = jnp.where(ahead == 0, 0, jnp.where(ahead <= 8, 2 * ahead - 1, 2 * (PLANES - ahead)))
            lane_keep = low if a % 2 == 0 else jnp.logical_not(low)
            even = jnp.logical_and(lane_keep, top)
            odd = jnp.logical_and(lane_keep, jnp.logical_not(top))
            for t in range(PAIRS):
                v = x[(i >> 1) & 1, o, t]
                f = flip(v)
                first = (i & 1) == 0
                e = jnp.where(first, v, f)
                d = jnp.where(first, f, v)
                for h in range(2):
                    same = h == a % 2
                    xa[q, 0, a * 10 + 2 * t + h] = jnp.where(even, e if same else turn(e), 0.0)
                    xa[q, 1, a * 10 + 2 * t + h] = jnp.where(odd, d if same else turn(d), 0.0)

    def rows_of(u):
        row = pl.multiple_of(16 * u, 16)
        for t in range(PAIRS):
            index = []
            for k in range(4):
                pair = [2 * t, 2 * t + 1] if 2 * t + 1 < ROWS else [2 * t]
                index.append([10 * a + tab[(4 * u + k - offs[a]) & (NB - 1)] for a in pair])
            for q in range(2):
                tiles = []
                for k in (0, 2):
                    v = xa[q, 0, index[k][0]] + xa[q, 1, index[k + 1][0]]
                    if len(index[k]) == 2:
                        v = v + (xa[q, 0, index[k][1]] + xa[q, 1, index[k + 1][1]])
                    tiles.append(v)
                hi, lo = split(jnp.concatenate(tiles, axis=0))
                ghi[q, pl.ds(row, 16), t * LANES:(t + 1) * LANES] = hi
                glo[q, pl.ds(row, 16), t * LANES:(t + 1) * LANES] = lo

    times(0, NB // 4, rows_of)
    for q in range(2):
        g = (ghi[q], glo[q])
        tmat = dot3(g, split(bm[q]))
        tt[q] = jnp.concatenate([tmat, tmat], axis=1).reshape(32, 8, LANES)
        cube = dot3(split(tmat.T), g)
        for t in range(PAIRS):
            w = cube[:, t * LANES:(t + 1) * LANES].T
            wide[q, t] = jnp.concatenate([w[:64], w[64:]], axis=1).reshape(8, 8, LANES)
    for t in range(PAIRS):
        for w in range(8):
            u, v = wide[0, t, w], wide[1, t, w]
            ct[2 * w, t] = jnp.where(top, u, flip(v))
            ct[2 * w + 1, t] = jnp.where(top, flip(u), v)
        parts = []
        for q in range(2):
            for h in range(2):
                a = 2 * t + h
                if a == ROWS:
                    parts.append(jnp.zeros((8, LANES), F32))
                    continue
                v = tt[q, offs[a] >> 1]
                parts.append(jnp.where((offs[a] & 1) == q, v, flip(v)))
        sq[t] = quadrants(*parts)


def kernel(
    dens, pat_hbm, order_hbm, out,
    pat, order, tab, landed, own, x_a, x_b, bbuf, ct, sq, rs, xa, ghi, glo, bm, tt, wide, dup, fsend, frecv,
    load, p_send, p_recv, z_send, z_recv, sib_send, sib_recv, b_send, b_recv, rs_send, rs_recv, f_send, f_recv,
):
    at = Place()
    x = (x_a, x_b)
    tables = (
        pltpu.make_async_copy(pat_hbm, pat, load.at[1]),
        pltpu.make_async_copy(order_hbm, order, load.at[2]),
    )
    for copy in tables:
        copy.start()
    greet_along(at)
    for *_, dev in at.cores():
        signal(dev)
    met(DEVS - 1 + 2 * len(JUMPS))
    scatter(at, dens, pat, order, tab, landed, own.at[0], tables, load.at[0], p_send, p_recv)
    for k in range(2):
        spread(
            at, own.at[k], x[k], bbuf.at[k], bm, z_send.at[k], z_recv.at[k], sib_send.at[k], sib_recv.at[k],
            b_send.at[k], b_recv.at[k],
        )
        product(at, x[k], tab, ct.at[k], sq, xa, ghi, glo, bm, tt, wide)
        reduce_slices(at, ct.at[k], sq, rs.at[k], own.at[k + 1], rs_send.at[k], rs_recv.at[k])
    finish(at, order, tab, out, own.at[2], dup, fsend, frecv, f_send, f_recv)
    take(landed.at[pl.ds(0, 2 * (DEVS - 1))], p_send)
    for k in range(2):
        take(x[k].at[0, pl.ds(0, PLANES - 1)], z_send.at[k])
        take(x[k].at[0], sib_send.at[k])
        take(bbuf.at[k, pl.ds(0, CHIPS - 1)], b_send.at[k])
        take(rs.at[k, pl.ds(0, CHIPS - 1)], rs_send.at[k])
    take(frecv.at[pl.ds(0, DEVS - 1)], f_send)


VM = pl.BlockSpec(memory_space=pltpu.VMEM)
HBM = pl.BlockSpec(memory_space=pltpu.HBM)
DMA = pltpu.SemaphoreType.DMA


def vmem(*dims, dtype=F32):
    return pltpu.VMEM(dims, dtype)


def local(density, pattern, grid_order):
    inputs = (density.reshape(2, 8, 8, 256), pattern.T, grid_order)
    out = pl.pallas_call(
        kernel,
        out_shape=jax.ShapeDtypeStruct((2, 8, 8, 256), F32),
        in_specs=[HBM, HBM, HBM],
        out_specs=VM,
        scratch_shapes=[
            pltpu.SMEM((ROWS, NB), jnp.int32), pltpu.SMEM((NB,), jnp.int32), pltpu.SMEM((TABLE,), jnp.int32),
            vmem(NB, 4, LANES), vmem(3, *CHUNK),
            vmem(2, PLANES, *CHUNK), vmem(2, PLANES, *CHUNK), vmem(2, CHIPS, *CHUNK), vmem(2, CHIPS, *CHUNK), vmem(*CHUNK),
            vmem(2, CHIPS, *CHUNK),
            vmem(2, 2, ROWS * 10, 8, LANES), vmem(2, 4 * NB, WIDE, dtype=BF16), vmem(2, 4 * NB, WIDE, dtype=BF16),
            vmem(2, WIDE, 64), vmem(2, 32, 8, LANES), vmem(2, PAIRS, 8, 8, LANES),
            vmem(10, 8, LANES), vmem(DEVS, 8, LANES), vmem(DEVS, 8, LANES),
            DMA((3,)), DMA, DMA, DMA((2,)), DMA((2, PLANES)), DMA((2,)), DMA((2,)), DMA((2,)), DMA((2,)), DMA((2,)), DMA((2,)),
            DMA, DMA,
        ],
        compiler_params=pltpu.CompilerParams(collective_id=0, has_side_effects=True, vmem_limit_bytes=16 << 20),
    )(*(pltpu.with_memory_space_constraint(v, pltpu.HBM) for v in inputs))
    return out.reshape(128, 256)


def solution(mesh):
    in_specs = (P(("col", "rep"), "row"), P(), P())
    out_specs = P(("col", "rep"), "row")
    return jax.shard_map(local, mesh=mesh, in_specs=in_specs, out_specs=out_specs, check_vma=False)
```

```python
import jax
import jax.numpy as jnp
from jax import lax
from jax.experimental import pallas as pl
from jax.experimental.pallas import tpu as pltpu
from jax.sharding import PartitionSpec as P

MESH = pl.DeviceIdType.MESH
F32 = jnp.float32
BF16 = jnp.bfloat16
PLANES = 16
CHIPS = 16
DEVS = 32
NB = 64
ROWS = 9
PAIRS = 5
LANES = 128
WIDE = PAIRS * LANES
CHUNK = (PAIRS, 8, LANES)
POS = NB
OFF = POS + 2 * ROWS
TABLE = 96

PARENT = {1: 0, 2: 0, 4: 0, 3: 4, 5: 4, 6: 4, 7: 4}
FIRST = (4, 2, 1)
ONWARD = (7, 6, 3, 5)
ARRIVAL = (1, 2, 4, 5, 3, 6, 7)
JUMPS = (4, 3, 2, 1)
SPOTS = sorted(
    ((dx, dy) for dx in range(4) for dy in range(4) if dx or dy),
    key=lambda o: -(min(o[0], 4 - o[0]) + min(o[1], 4 - o[1])),
)


class Place:
    def __init__(self):
        self.r = lax.axis_index("row")
        self.c = lax.axis_index("col")
        self.p = lax.axis_index("rep")
        self.me = self.c * 4 + self.p
        self.core = self.c % 2
        self.chip = (self.c // 2) * 4 + self.p
        self.sibling = (self.r, self.c + 1 - 2 * self.core, self.p)

    def along(self, d):
        return (lax.rem(self.r + d + PLANES, PLANES), self.c, self.p)

    def spot(self, dx, dy):
        return lax.rem(self.c // 2 + dx, 4), lax.rem(self.p + dy, 4)

    def other(self, o):
        x, y = self.spot(*o)
        return x * 4 + y, (self.r, x * 2 + self.core, y)

    def cores(self):
        for dx, dy in SPOTS:
            x, y = self.spot(dx, dy)
            for h in range(2):
                yield x, y, h, (self.r, x * 2 + h, y)
        yield self.c // 2, self.p, 1 - self.core, self.sibling


def put(src, dst, ssem, rsem, dev):
    pltpu.make_async_remote_copy(
        src_ref=src, dst_ref=dst, send_sem=ssem, recv_sem=rsem, device_id=dev, device_id_type=MESH
    ).start()


def take(ref, sem):
    pltpu.make_async_copy(ref, ref, sem).wait()


def signal(dev):
    pl.semaphore_signal(pltpu.get_barrier_semaphore(), inc=1, device_id=dev, device_id_type=MESH)


def met(n):
    pl.semaphore_wait(pltpu.get_barrier_semaphore(), n)


def times(first, last, body):
    def step(t, carry):
        body(t)
        return carry

    lax.fori_loop(first, last, step, 0)


def greet_along(at):
    for d in JUMPS:
        signal(at.along(d))
        signal(at.along(-d))


def lane_low():
    return lax.broadcasted_iota(jnp.int32, (8, LANES), 1) < 64


def row_low():
    return lax.broadcasted_iota(jnp.int32, (8, LANES), 0) < 4


def turn(v):
    return pltpu.roll(v, 64, 1)


def flip(v):
    return pltpu.roll(v, 4, 0)


def quadrants(q00, q01, q10, q11):
    low = lane_low()
    return jnp.where(row_low(), jnp.where(low, q00, q01), jnp.where(low, q10, q11))


def block_columns(bbuf, bm):
    top = row_low()
    for q in range(2):
        for t in range(PAIRS):
            for w in range(8):
                u, v = bbuf[2 * w, t], bbuf[2 * w + 1, t]
                v = jnp.where(top, u, flip(v)) if q == 0 else jnp.where(top, flip(u), v)
                bm[q, 128 * t + 8 * w:128 * t + 8 * w + 8] = v[:, :64]
                bm[q, 128 * t + 64 + 8 * w:128 * t + 72 + 8 * w] = v[:, 64:]


def spread(at, own, x, bbuf, bm, z_send, z_recv, sib_send, sib_recv, b_send, b_recv):
    mine = x.at[at.core]

    def slot(sign, q):
        return 2 * q - 1 if sign > 0 else 2 * q

    def send(src, sign, q):
        o = slot(sign, q)
        put(src, mine.at[o], z_send, z_recv.at[o], at.along(sign * (q - PARENT[q])))

    for q in FIRST:
        for sign in (1, -1):
            send(own, sign, q)

    for o in SPOTS:
        put(own, bbuf.at[at.chip], b_send, b_recv, at.other(o)[1])
    put(own, mine.at[0], sib_send, sib_recv, at.sibling)
    x[at.core, 0] = own[...]
    bbuf[at.chip] = own[...]
    side = 1 - 2 * at.core
    for q in ARRIVAL:
        for sign in (1, -1):
            take(mine.at[slot(sign, q)], z_recv.at[slot(sign, q)])
        if q == 4:
            put(mine.at[7 + at.core], mine.at[15], z_send, z_recv.at[15], at.along(4 * side))
        for k in ONWARD:
            if PARENT[k] == q:
                for sign in (1, -1):
                    send(mine.at[slot(sign, q)], sign, k)
        for sign in (1, -1):
            part = mine.at[slot(sign, q)]
            put(part, part, sib_send, sib_recv, at.sibling)
        if q == 4:
            take(bbuf.at[pl.ds(0, CHIPS - 1)], b_recv)
            block_columns(bbuf, bm)
    last = mine.at[15]
    take(last, z_recv.at[15])
    put(last, last, sib_send, sib_recv, at.sibling)
    take(x.at[1 - at.core], sib_recv)


def fill_tables(at, pat, order, tab, near, dense):
    offs = [pat[a, 0] for a in range(ROWS)]
    targets = [(order[4 * at.r + 2 * at.core + q] + off) & (NB - 1) for q in range(2) for off in offs]

    def step(o, found):
        v = jnp.int32(ROWS)
        for a in range(ROWS):
            v = jnp.where(offs[a] == o, jnp.int32(a), v)
        tab[o] = v
        n = order[o]
        return tuple(jnp.where(n == target, o, f) for target, f in zip(targets, found))

    found = lax.fori_loop(0, NB, step, (jnp.int32(0),) * len(targets))
    for k, f in enumerate(found):
        tab[POS + k] = f
    for a in range(ROWS):
        tab[OFF + a] = offs[a]
    natural = [order[4 * at.r + 2 * at.core + q] for q in range(2)]

    def look(o):
        for a in range(ROWS):
            near[o * ROWS + a] = 10 * a + tab[(o - offs[a]) & (NB - 1)]
        for q in range(2):
            dense[q * NB + o] = tab[(order[o] - natural[q]) & (NB - 1)]

    times(0, NB, look)


def scatter(at, dens, pat, order, tab, near, dense, landed, own, tables, load, p_send, p_recv):
    def lanes(c):
        return pl.ds(pl.multiple_of((c % 2) * LANES, LANES), LANES)

    own_part = pltpu.make_async_copy(
        dens.at[:, at.chip // 2, pl.ds(4 * (at.p % 2), 4), lanes(at.c)], landed.at[pl.ds(2 * at.me, 2)], load
    )
    own_part.start()
    for x, y, h, dev in at.cores():
        put(dens.at[:, x * 2 + y // 2, pl.ds(4 * (y % 2), 4), lanes(h)], landed.at[pl.ds(2 * at.me, 2)], p_send, p_recv, dev)
    for copy in (*tables, own_part):
        copy.wait()
    fill_tables(at, pat, order, tab, near, dense)
    take(landed.at[pl.ds(0, 2 * (DEVS - 1))], p_recv)
    for t in range(PAIRS):
        parts = []
        for q in range(2):
            for h in range(2):
                a = 2 * t + h
                if a == ROWS:
                    parts.append(jnp.zeros((8, LANES), F32))
                    continue
                v = landed[tab[POS + q * ROWS + a]]
                v = jnp.concatenate([v, v], axis=0)
                parts.append(v if h == q else turn(v))
        own[t] = quadrants(*parts)


def reduce_slices(at, ct, sq, rs, own, send, recv):
    for o in SPOTS:
        d, dev = at.other(o)
        put(ct.at[d], rs.at[at.chip], send, recv, dev)
    rs[at.chip] = ct[at.chip]
    take(rs.at[pl.ds(0, CHIPS - 1)], recv)
    for t in range(PAIRS):
        acc = rs[0, t]
        for k in range(1, CHIPS):
            acc = acc + rs[k, t]
        own[t] = 3.0 * sq[t] - 2.0 * acc


def finish(at, dense, out, own, dup, fsend, frecv, send, recv):
    low = lane_low()
    for t in range(PAIRS):
        v = own[t]
        w = turn(v)
        dup[2 * t] = jnp.where(low, v, w)
        dup[2 * t + 1] = jnp.where(low, w, v)

    def rows_for(d):
        fsend[d] = quadrants(*(dup[dense[q * NB + 2 * d + b]] for q in range(2) for b in range(2)))

    times(0, DEVS, rows_for)

    for x, y, h, dev in at.cores():
        put(fsend.at[(x * 2 + h) * 4 + y], frecv.at[at.chip * 2 + at.core], send, recv, dev)
    frecv[at.chip * 2 + at.core] = fsend[at.me]
    rest = frecv.at[pl.ds(0, DEVS - 1)]
    take(rest, recv)
    for b in range(2):
        for w in range(8):
            for h in range(2):
                parts = []
                for sp in range(2):
                    for q in range(2):
                        v = frecv[(2 * w + sp) * 2 + h]
                        v = v if q == b else turn(v)
                        parts.append(v if q == sp else flip(v))
                out[b, w, :, h * LANES:(h + 1) * LANES] = quadrants(*parts)


def split(v):
    hi = v.astype(BF16)
    return hi, (v - hi.astype(F32)).astype(BF16)


def dot3(a, b):
    def one(u, v):
        return jnp.dot(u, v, preferred_element_type=F32)

    return one(a[0], b[0]) + (one(a[0], b[1]) + one(a[1], b[0]))


def product(at, x, tab, near, ct, sq, xa, ghi, glo, bm, tt, wide):
    low = lane_low()
    top = row_low()
    offs = [tab[OFF + a] for a in range(ROWS)]
    for q in range(2):
        for a in range(ROWS):
            i = tab[POS + q * ROWS + a]
            ahead = (at.r - (i >> 2)) & (PLANES - 1)
            o = jnp.where(ahead == 0, 0, jnp.where(ahead <= 8, 2 * ahead - 1, 2 * (PLANES - ahead)))
            lane_keep = low if a % 2 == 0 else jnp.logical_not(low)
            even = jnp.logical_and(lane_keep, top)
            odd = jnp.logical_and(lane_keep, jnp.logical_not(top))
            for t in range(PAIRS):
                v = x[(i >> 1) & 1, o, t]
                f = flip(v)
                first = (i & 1) == 0
                e = jnp.where(first, v, f)
                d = jnp.where(first, f, v)
                for h in range(2):
                    same = h == a % 2
                    xa[q, 0, a * 10 + 2 * t + h] = jnp.where(even, e if same else turn(e), 0.0)
                    xa[q, 1, a * 10 + 2 * t + h] = jnp.where(odd, d if same else turn(d), 0.0)

    def rows_of(u):
        row = pl.multiple_of(16 * u, 16)
        for t in range(PAIRS):
            index = []
            for k in range(4):
                pair = [2 * t, 2 * t + 1] if 2 * t + 1 < ROWS else [2 * t]
                index.append([near[(4 * u + k) * ROWS + a] for a in pair])
            for q in range(2):
                tiles = []
                for k in (0, 2):
                    v = xa[q, 0, index[k][0]] + xa[q, 1, index[k + 1][0]]
                    if len(index[k]) == 2:
                        v = v + (xa[q, 0, index[k][1]] + xa[q, 1, index[k + 1][1]])
                    tiles.append(v)
                hi, lo = split(jnp.concatenate(tiles, axis=0))
                ghi[q, pl.ds(row, 16), t * LANES:(t + 1) * LANES] = hi
                glo[q, pl.ds(row, 16), t * LANES:(t + 1) * LANES] = lo

    times(0, NB // 4, rows_of)
    for q in range(2):
        g = (ghi[q], glo[q])
        tmat = dot3(g, split(bm[q]))
        tt[q] = jnp.concatenate([tmat, tmat], axis=1).reshape(32, 8, LANES)
        cube = dot3(split(tmat.T), g)
        for t in range(PAIRS):
            w = cube[:, t * LANES:(t + 1) * LANES].T
            wide[q, t] = jnp.concatenate([w[:64], w[64:]], axis=1).reshape(8, 8, LANES)
    for t in range(PAIRS):
        for w in range(8):
            u, v = wide[0, t, w], wide[1, t, w]
            ct[2 * w, t] = jnp.where(top, u, flip(v))
            ct[2 * w + 1, t] = jnp.where(top, flip(u), v)
        parts = []
        for q in range(2):
            for h in range(2):
                a = 2 * t + h
                if a == ROWS:
                    parts.append(jnp.zeros((8, LANES), F32))
                    continue
                v = tt[q, offs[a] >> 1]
                parts.append(jnp.where((offs[a] & 1) == q, v, flip(v)))
        sq[t] = quadrants(*parts)


def kernel(
    dens, pat_hbm, order_hbm, out,
    pat, order, tab, near, dense, landed, own, x_a, x_b, bbuf, ct, sq, rs, xa, ghi, glo, bm, tt, wide, dup, fsend, frecv,
    load, p_send, p_recv, z_send, z_recv, sib_send, sib_recv, b_send, b_recv, rs_send, rs_recv, f_send, f_recv,
):
    at = Place()
    x = (x_a, x_b)
    tables = (
        pltpu.make_async_copy(pat_hbm, pat, load.at[1]),
        pltpu.make_async_copy(order_hbm, order, load.at[2]),
    )
    for copy in tables:
        copy.start()
    greet_along(at)
    for *_, dev in at.cores():
        signal(dev)
    met(DEVS - 1 + 2 * len(JUMPS))
    scatter(at, dens, pat, order, tab, near, dense, landed, own.at[0], tables, load.at[0], p_send, p_recv)
    for k in range(2):
        spread(
            at, own.at[k], x[k], bbuf.at[k], bm, z_send.at[k], z_recv.at[k], sib_send.at[k], sib_recv.at[k],
            b_send.at[k], b_recv.at[k],
        )
        product(at, x[k], tab, near, ct.at[k], sq, xa, ghi, glo, bm, tt, wide)
        reduce_slices(at, ct.at[k], sq, rs.at[k], own.at[k + 1], rs_send.at[k], rs_recv.at[k])
    finish(at, dense, out, own.at[2], dup, fsend, frecv, f_send, f_recv)
    take(landed.at[pl.ds(0, 2 * (DEVS - 1))], p_send)
    for k in range(2):
        take(x[k].at[0, pl.ds(0, PLANES - 1)], z_send.at[k])
        take(x[k].at[0], sib_send.at[k])
        take(bbuf.at[k, pl.ds(0, CHIPS - 1)], b_send.at[k])
        take(rs.at[k, pl.ds(0, CHIPS - 1)], rs_send.at[k])
    take(frecv.at[pl.ds(0, DEVS - 1)], f_send)


VM = pl.BlockSpec(memory_space=pltpu.VMEM)
HBM = pl.BlockSpec(memory_space=pltpu.HBM)
DMA = pltpu.SemaphoreType.DMA


def vmem(*dims, dtype=F32):
    return pltpu.VMEM(dims, dtype)


def local(density, pattern, grid_order):
    inputs = (density.reshape(2, 8, 8, 256), pattern.T, grid_order)
    out = pl.pallas_call(
        kernel,
        out_shape=jax.ShapeDtypeStruct((2, 8, 8, 256), F32),
        in_specs=[HBM, HBM, HBM],
        out_specs=VM,
        scratch_shapes=[
            pltpu.SMEM((ROWS, NB), jnp.int32), pltpu.SMEM((NB,), jnp.int32), pltpu.SMEM((TABLE,), jnp.int32),
            pltpu.SMEM((NB * ROWS,), jnp.int32), pltpu.SMEM((2 * NB,), jnp.int32),
            vmem(NB, 4, LANES), vmem(3, *CHUNK),
            vmem(2, PLANES, *CHUNK), vmem(2, PLANES, *CHUNK), vmem(2, CHIPS, *CHUNK), vmem(2, CHIPS, *CHUNK), vmem(*CHUNK),
            vmem(2, CHIPS, *CHUNK),
            vmem(2, 2, ROWS * 10, 8, LANES), vmem(2, 4 * NB, WIDE, dtype=BF16), vmem(2, 4 * NB, WIDE, dtype=BF16),
            vmem(2, WIDE, 64), vmem(2, 32, 8, LANES), vmem(2, PAIRS, 8, 8, LANES),
            vmem(10, 8, LANES), vmem(DEVS, 8, LANES), vmem(DEVS, 8, LANES),
            DMA((3,)), DMA, DMA, DMA((2,)), DMA((2, PLANES)), DMA((2,)), DMA((2,)), DMA((2,)), DMA((2,)), DMA((2,)), DMA((2,)),
            DMA, DMA,
        ],
        compiler_params=pltpu.CompilerParams(collective_id=0, has_side_effects=True, vmem_limit_bytes=16 << 20),
    )(*(pltpu.with_memory_space_constraint(v, pltpu.HBM) for v in inputs))
    return out.reshape(128, 256)


def solution(mesh):
    in_specs = (P(("col", "rep"), "row"), P(), P())
    out_specs = P(("col", "rep"), "row")
    return jax.shard_map(local, mesh=mesh, in_specs=in_specs, out_specs=out_specs, check_vma=False)
```
